32 devices in a mesh: stream: 8 (over z, x), span: 4 (over y, core).
Axes of the slice: x: 2, y: 2, z: 4, core: 2. Of those that a mesh axis runs over, the one named last changes fastest.
Arguments:
- state: float32 [5, 8, 128, 512], P(None, None, 'stream', 'span'), may hold values from -0.3 to 3, as said below
Outputs:
- state_next: float32 [5, 8, 128, 512], P(None, None, 'stream', 'span')
- flux_difference: float32 [5, 8, 128, 512], P(None, None, 'stream', 'span')
The draws below stay inside these ranges and needn't reach their ends.
Inputs may be any that keep to these rules, and one draw needn't show every extreme that they name: Each cell holds a gas state with density from 0.55 to 1.65, streamwise velocity from 0.2 to 0.6, spanwise and wall-normal velocities within 0.15 of zero and pressure from 0.55 to 1.0.
All inputs are finite; a program needn't handle non-finite values.
Results may differ from the reference program's by a relative error of at most 0.002.
Values sent between devices are 32-bit elements; how exact they have to be, the bound alone decides.
No kernel may reach another device: no remote copies, remote signals or barrier semaphores. Data moves between devices by JAX's collectives and lax.ppermute only.
A program may use at most 128 MiB of HBM per device.

```python
import jax
import jax.numpy as jnp
from jax import lax

CX = 16
NZ = 8
NX = 128
NY = 512


def draw_state(key, part):
    folded = jax.random.fold_in(key, 7)
    subkeys = jax.random.split(folded, 6)
    grid_shape = (NZ, NX, NY)
    uniforms = [jax.random.uniform(subkeys[field_id], grid_shape, jnp.float32) for field_id in range(5)]
    density = 0.6 + 0.8 * uniforms[0]
    speed_x = 0.25 + 0.3 * uniforms[1]
    pressure = 0.6 + 0.4 * uniforms[4]
    speed_y = 0.3 * (uniforms[2] - 0.5)
    speed_z = 0.3 * (uniforms[3] - 0.5)
    energy = pressure / 0.4 + 0.5 * density * (speed_x * speed_x + speed_y * speed_y + speed_z * speed_z)
    return jnp.stack([density, density * speed_x, density * speed_y, density * speed_z, energy])


def setup_inputs(seed: int = 0) -> dict:
    streams_of = jax.random.split(jax.random.key(seed), 2)
    state = draw_state(jax.random.fold_in(streams_of[1], 71), 0)
    return dict(state=state)


GAMMA = 1.4
GAMMA_LESS = 0.4
DAMPING = 0.125
DIAGONAL = 1.25

def primitives(fields):
    density = fields[0]
    speed_x = fields[1] / density
    speed_y = fields[2] / density
    speed_z = fields[3] / density
    kinetic = 0.5 * (speed_x * speed_x + speed_y * speed_y + speed_z * speed_z)
    pressure = GAMMA_LESS * (fields[4] - density * kinetic)
    return (density, speed_x, speed_y, speed_z, kinetic, pressure)

def flux_along(fields, direction):
    density, speed_x, speed_y, speed_z, kinetic, pressure = primitives(fields)
    normal_speed = (speed_x, speed_y, speed_z)[direction - 1]
    mass_flow = density * normal_speed
    columns = [mass_flow, mass_flow * speed_x, mass_flow * speed_y, mass_flow * speed_z, normal_speed * (fields[4] + pressure)]
    columns[direction] = columns[direction] + pressure
    return jnp.stack(columns)

def jacobian_rows(fields):
    density, speed_x, speed_y, speed_z, kinetic, pressure = primitives(fields)
    enthalpy = (fields[4] + pressure) / density
    zero_entry = jnp.zeros_like(density)
    unit_entry = jnp.ones_like(density)
    gas_kinetic = GAMMA_LESS * kinetic
    return [[zero_entry, unit_entry, zero_entry, zero_entry, zero_entry], [gas_kinetic - speed_x * speed_x, (3.0 - GAMMA) * speed_x, -GAMMA_LESS * speed_y, -GAMMA_LESS * speed_z, GAMMA_LESS * unit_entry], [-speed_x * speed_y, speed_y, speed_x, zero_entry, zero_entry], [-speed_x * speed_z, speed_z, zero_entry, speed_x, zero_entry], [speed_x * (gas_kinetic - enthalpy), enthalpy - GAMMA_LESS * speed_x * speed_x, -GAMMA_LESS * speed_x * speed_y, -GAMMA_LESS * speed_x * speed_z, GAMMA * speed_x]]

def jacobian(fields):
    return jnp.stack([jnp.stack(matrix_row) for matrix_row in jacobian_rows(fields)])

def jacobian_apply(fields, vector):
    result = []
    for matrix_row in jacobian_rows(fields):
        running_sum = matrix_row[0] * vector[0]
        for column in range(1, 5):
            running_sum = running_sum + matrix_row[column] * vector[column]
        result.append(running_sum)
    return jnp.stack(result)

def matmul_small(left_block, right_block):
    return lax.optimization_barrier(jnp.sum(left_block[:, :, None] * right_block[None], axis=1))

def identity_like(matrix):
    return jnp.eye(5, dtype=matrix.dtype).reshape((5, 5) + (1,) * (matrix.ndim - 2))

def solve_small(matrix, targets):
    normal_matrix = {}
    for row_id in range(5):
        for col_id in range(row_id + 1):
            normal_matrix[row_id, col_id] = lax.optimization_barrier(jnp.sum(matrix[:, row_id] * matrix[:, col_id], axis=0))
    projected = [lax.optimization_barrier(jnp.sum(matrix[:, row_id][:, None] * targets, axis=0)) for row_id in range(5)]
    factor_entries = {}
    inverse = []
    for row_id in range(5):
        for col_id in range(row_id + 1):
            current = normal_matrix[row_id, col_id]
            for mid_id in range(col_id):
                current = current - factor_entries[row_id, mid_id] * factor_entries[col_id, mid_id]
            if row_id == col_id:
                inverse.append(1.0 / jnp.sqrt(current))
            else:
                factor_entries[row_id, col_id] = current * inverse[col_id]
    forward = []
    for row_id in range(5):
        current = projected[row_id]
        for mid_id in range(row_id):
            current = current - factor_entries[row_id, mid_id][None] * forward[mid_id]
        forward.append(current * inverse[row_id][None])
    solution = [None] * 5
    for row_id in reversed(range(5)):
        current = forward[row_id]
        for mid_id in range(row_id + 1, 5):
            current = current - factor_entries[mid_id, row_id][None] * solution[mid_id]
        solution[row_id] = current * inverse[row_id][None]
    return jnp.stack(solution)

def thomas_step(running, inputs):
    factor, partial_value = running
    near_block, far_block, source = inputs
    pivot_block = DIAGONAL * identity_like(near_block) - matmul_small(near_block, factor)
    columns = jnp.concatenate([far_block, source - matmul_small(near_block, partial_value)], axis=1)
    solved = solve_small(pivot_block, columns)
    updated = (solved[:, :5], solved[:, 5:])
    return (updated, updated)

def back_step(following, inputs):
    factor, partial_value = inputs
    current = partial_value - matmul_small(factor, following)
    return (current, current)

def couplings(ext_plane, courant):
    blocks = jacobian(ext_plane)
    identity_block = identity_like(blocks)
    lower_rows = -(0.5 * courant) * blocks[:, :, :-2] - DAMPING * identity_block
    upper_rows = 0.5 * courant * blocks[:, :, 2:] - DAMPING * identity_block
    return (jnp.moveaxis(lower_rows, 2, 0), jnp.moveaxis(upper_rows, 2, 0))

def right_side(state, stream_padded, flux_padded, span_padded, courant):
    flux_step = flux_padded[:, :, 2:] - flux_padded[:, :, :-2]
    curvature = stream_padded[:, :, 2:] - 2.0 * state + stream_padded[:, :, :-2]
    span_flux = flux_along(span_padded, 2)
    span_step = (-span_flux[..., 4:] + 8.0 * span_flux[..., 3:-1] - 8.0 * span_flux[..., 1:-3] + span_flux[..., :-4]) / 12.0
    mirror = jnp.array([1.0, 1.0, 1.0, -1.0, 1.0], dtype=state.dtype).reshape(5, 1, 1, 1)
    normal_padded = jnp.concatenate([state[:, :1] * mirror, state, state[:, -1:]], axis=1)
    normal_flux = flux_along(normal_padded, 3)
    normal_step = 0.5 * (normal_flux[:, 2:] - normal_flux[:, :-2])
    return -(0.5 * courant) * flux_step + DAMPING * curvature - span_step - normal_step

def reference(state):
    courant = 4.0 * CX
    widths = ((0, 0), (0, 0), (1, 1), (0, 0))
    stream_padded = jnp.pad(state, widths)
    flux_padded = jnp.pad(flux_along(state, 1), widths)
    span_padded = jnp.concatenate([state[..., -2:], state, state[..., :2]], axis=3)
    source = right_side(state, stream_padded, flux_padded, span_padded, courant)
    resting = jnp.array([1.0, 0.0, 0.0, 0.0, 2.5], dtype=state.dtype).reshape(5, 1, 1, 1)
    resting = jnp.broadcast_to(resting, (5, state.shape[1], 1, state.shape[3]))
    extended = jnp.concatenate([resting, state, resting], axis=2)

    def solve_plane(plane_inputs):
        ext_plane, source_plane = plane_inputs
        lower_rows, upper_rows = couplings(ext_plane, courant)
        source_rows = jnp.moveaxis(source_plane, 1, 0)[:, :, None]
        start = (jnp.zeros_like(lower_rows[0]), jnp.zeros_like(source_rows[0]))
        ignored, stored = lax.scan(thomas_step, start, (lower_rows, upper_rows, source_rows))
        ignored_last, values = lax.scan(back_step, jnp.zeros_like(source_rows[0]), stored, reverse=True)
        return jnp.moveaxis(values[:, :, 0], 0, 1)
    update = lax.map(solve_plane, (jnp.moveaxis(extended, 1, 0), jnp.moveaxis(source, 1, 0)))
    update = jnp.moveaxis(update, 0, 1)
    state_next = state + update
    linear_flux = jacobian_apply(state, state_next)
    linear_padded = jnp.pad(linear_flux, widths)
    flux_difference = -0.5 * (linear_padded[:, :, 2:] - linear_padded[:, :, :-2])
    return (state_next, flux_difference)
```

```python
import functools

import jax
import jax.numpy as jnp
from jax import lax
from jax.experimental import pallas as pl
from jax.experimental.pallas import tpu as pltpu
from jax.sharding import PartitionSpec as P

GAMMA = 1.4
GAMMA_LESS = 0.4
DAMPING = 0.125
DIAGONAL = 1.25

SIDE = 55
STATES = 110
PORT = 120


def add(a, b):
    return b if a is None else a if b is None else a + b


def sub(a, b):
    return a if b is None else -b if a is None else a - b


def mul(a, b):
    return None if a is None or b is None else a * b


def vadd(a, b):
    return [add(x, y) for x, y in zip(a, b)]


def matvec(cols, vec):
    out = []
    for row in range(5):
        acc = None
        for col in range(5):
            acc = add(acc, mul(cols[col][row], vec[col]))
        out.append(acc)
    return out


def factorize(rows):
    rows = [list(row) for row in rows]
    inverse = [None] * 5
    for k in range(5):
        inverse[k] = 1.0 / rows[k][k]
        for i in range(k + 1, 5):
            rows[i][k] = rows[i][k] * inverse[k]
            for j in range(k + 1, 5):
                rows[i][j] = sub(rows[i][j], mul(rows[i][k], rows[k][j]))
    return rows, inverse


def resolve(factors, vec):
    rows, inverse = factors
    x = list(vec)
    for i in range(5):
        for k in range(i):
            x[i] = sub(x[i], mul(rows[i][k], x[k]))
    for i in reversed(range(5)):
        for k in range(i + 1, 5):
            x[i] = sub(x[i], mul(rows[i][k], x[k]))
        x[i] = mul(x[i], inverse[i])
    return x


def primitives(fields):
    density, mom_x, mom_y, mom_z, energy = fields
    inverse = 1.0 / density
    u, v, w = mom_x * inverse, mom_y * inverse, mom_z * inverse
    kinetic = 0.5 * (u * u + v * v + w * w)
    pressure = GAMMA_LESS * (energy - density * kinetic)
    return u, v, w, kinetic, pressure, inverse


def differences(here, there):
    du, dv, dw = (b - a for a, b in zip(here[:3], there[:3]))
    half_square = 0.5 * GAMMA_LESS * (du * du + dv * dv + dw * dw)
    return du, dv, dw, half_square, GAMMA_LESS * du, GAMMA_LESS * dv, GAMMA_LESS * dw


def shift_frame(t, diff):
    du, dv, dw, half_square, du4, dv4, dw4 = diff
    return [
        t[0],
        t[1] + du * t[0],
        t[2] + dv * t[0],
        t[3] + dw * t[0],
        t[4] + half_square * t[0] + (du4 * t[1] + dv4 * t[2] + dw4 * t[3]),
    ]


def advect(x, speed, sound):
    return [
        speed * x[0] + x[1],
        speed * x[1] + x[4],
        speed * x[2],
        speed * x[3],
        speed * x[4] + sound * x[1],
    ]


def to_conserved(z, cell):
    u, v, w, kinetic = cell[:4]
    return [
        z[0],
        u * z[0] + z[1],
        v * z[0] + z[2],
        w * z[0] + z[3],
        kinetic * z[0] + u * z[1] + v * z[2] + w * z[3] + (1.0 / GAMMA_LESS) * z[4],
    ]


def to_primitive(x, cell):
    u, v, w, kinetic = cell[:4]
    return [
        x[0],
        x[1] - u * x[0],
        x[2] - v * x[0],
        x[3] - w * x[0],
        GAMMA_LESS * (kinetic * x[0] - u * x[1] - v * x[2] - w * x[3] + x[4]),
    ]


def primitive_columns(cell):
    u, v, w, kinetic = cell[:4]
    one = jnp.ones_like(u)
    return [
        [one, -u, -v, -w, GAMMA_LESS * kinetic],
        [None, one, None, None, -GAMMA_LESS * u],
        [None, None, one, None, -GAMMA_LESS * v],
        [None, None, None, one, -GAMMA_LESS * w],
        [None, None, None, None, GAMMA_LESS * one],
    ]


def upper_columns(diff, speed, sound):
    du, dv, dw, half_square, du4, dv4, dw4 = diff
    less = -speed
    one = jnp.ones_like(speed)
    return [
        [less, du * less, dv * less, dw * less, half_square * less],
        [-one, -(du + speed), -dv, -dw, du4 * less - (half_square + sound)],
        [None, None, less, None, dv4 * less],
        [None, None, None, less, dw4 * less],
        [None, -one, None, None, -(du4 + speed)],
    ]


def neighbour_value(coupling, fields, eps):
    u, v, w, kinetic, pressure, inverse = primitives(fields)
    z = to_primitive(coupling, (u, v, w, kinetic))
    speed = u + eps
    sound = GAMMA * pressure * inverse
    over = 1.0 / speed
    det = 1.0 / (speed * speed - sound)
    w1 = (speed * z[1] - z[4]) * det
    w4 = (speed * z[4] - sound * z[1]) * det
    return to_conserved([(z[0] - w1) * over, w1, z[2] * over, z[3] * over, w4], (u, v, w, kinetic))


def flux_along(fields, cell, direction):
    pressure = cell[4]
    normal = cell[direction - 1]
    columns = [normal * fields[m] for m in range(4)]
    columns.append(normal * (fields[4] + pressure))
    columns[direction] = columns[direction] + pressure
    return columns


def merge(low, high):
    a1, a2 = low
    b1, b2 = high
    product = [matvec(b1[:5], col) for col in a2[5:10]]
    one = jnp.ones_like(product[0][0])
    system = [[(one if r == c else 0.0) - product[c][r] for c in range(5)] for r in range(5)]
    factors = factorize(system)
    columns = [matvec(b1[:5], col) for col in a2[:5]] + b1[5:10]
    columns.append(vadd(matvec(b1[:5], a2[10]), b1[10]))
    down = [resolve(factors, col) for col in columns]
    up = [matvec(a2[5:10], col) for col in down]
    up = [vadd(up[c], a2[c]) for c in range(5)] + up[5:10] + [vadd(up[10], a2[10])]
    out1 = [matvec(a1[5:10], col) for col in down]
    out1 = [vadd(out1[c], a1[c]) for c in range(5)] + out1[5:10] + [vadd(out1[10], a1[10])]
    out2 = [matvec(b2[:5], col) for col in up]
    out2 = out2[:5] + [vadd(out2[c], b2[c]) for c in range(5, 10)] + [vadd(out2[10], b2[10])]
    return (out1, out2), down, up


def split_halves(value, bit):
    planes, lanes = value.shape
    if planes > 1:
        halves = value[: planes // 2], value[planes // 2 :]
    else:
        halves = value[:, : lanes // 2], value[:, lanes // 2 :]
    return jnp.where(bit == 0, halves[0], halves[1]), jnp.where(bit == 0, halves[1], halves[0])


def join_halves(kept, came, bit, planes):
    axis = 0 if planes > 1 else 1
    low = jnp.where(bit == 0, kept, came)
    high = jnp.where(bit == 0, came, kept)
    return jnp.concatenate([low, high], axis=axis)


def half_shape(shape):
    planes, lanes = shape
    return (planes // 2, lanes) if planes > 1 else (planes, lanes // 2)


def unpack_port(load):
    sides = [[[load(s * SIDE + 5 * c + r) for r in range(5)] for c in range(11)] for s in range(2)]
    first = [load(STATES + r) for r in range(5)]
    last = [load(STATES + 5 + r) for r in range(5)]
    return sides, first, last


def emit_split(keep_ref, send_ref, bit, sides, first, last):
    def emit(index, value):
        kept, sent = split_halves(value, bit)
        keep_ref[index] = kept
        send_ref[index] = sent

    for s in range(2):
        for c in range(11):
            for r in range(5):
                emit(s * SIDE + 5 * c + r, sides[s][c][r])
    for r in range(5):
        emit(STATES + r, first[r])
        emit(STATES + 5 + r, last[r])


def emit_facing(keep_ref, send_ref, bit, sides, first, last):
    for c in range(6):
        for r in range(5):
            as_low = sides[1][5 + c][r]
            as_high = sides[0][c if c < 5 else 10][r]
            value = jnp.where(bit == 0, as_low, as_high)
            keep_ref[5 * c + r] = value
            send_ref[5 * c + r] = value
    for r in range(5):
        value = jnp.where(bit == 0, last[r], first[r])
        keep_ref[30 + r] = value
        send_ref[30 + r] = value


def merge_kernel(level, top, bits_ref, own_ref, came_ref, keep_ref, send_ref, face_ref):
    bit = bits_ref[level]
    low = lambda e: jnp.where(bit == 0, own_ref[e], came_ref[e])
    high = lambda e: jnp.where(bit == 0, came_ref[e], own_ref[e])
    low_sides, first, low_last = unpack_port(low)
    high_sides, high_first, last = unpack_port(high)
    sides, down, up = merge(low_sides, high_sides)
    for c in range(11):
        for r in range(5):
            face_ref[5 * c + r] = down[c][r]
            face_ref[SIDE + 5 * c + r] = up[c][r]
    for r in range(5):
        face_ref[STATES + r] = low_last[r]
        face_ref[STATES + 5 + r] = high_first[r]
    emit = emit_facing if top else emit_split
    emit(keep_ref, send_ref, bits_ref[level + 1], sides, first, last)


def descend(bit, face_ref, values, eps, own_ref, partner_ref):
    low_in, high_in, low_n, high_n = values
    down, up = (
        [[face_ref[s * SIDE + 5 * c + r] for r in range(5)] for c in range(11)] for s in range(2)
    )
    from_high = vadd(vadd(matvec(down[:5], low_in), matvec(down[5:10], high_in)), down[10])
    from_low = vadd(vadd(matvec(up[:5], low_in), matvec(up[5:10], high_in)), up[10])
    low_last = [face_ref[STATES + r] for r in range(5)]
    high_first = [face_ref[STATES + 5 + r] for r in range(5)]
    n_low = neighbour_value(from_low, low_last, eps)
    n_high = neighbour_value([-e for e in from_high], high_first, -eps)
    as_low = low_in + from_high + low_n + n_high
    as_high = from_low + high_in + n_low + high_n
    for e in range(20):
        own_ref[e] = jnp.where(bit == 0, as_low[e], as_high[e])
        partner_ref[e] = jnp.where(bit == 0, as_high[e], as_low[e])


def top_kernel(level, eps, bits_ref, own_ref, came_ref, face_ref, own_out, partner_out):
    bit = bits_ref[level]
    low = [jnp.where(bit == 0, own_ref[e], came_ref[e]) for e in range(35)]
    high = [jnp.where(bit == 0, came_ref[e], own_ref[e]) for e in range(35)]
    low_cols = [low[5 * c : 5 * c + 5] for c in range(6)]
    high_cols = [high[5 * c : 5 * c + 5] for c in range(6)]
    product = [matvec(high_cols[:5], col) for col in low_cols[:5]]
    system = [[(1.0 if r == c else 0.0) - product[c][r] for c in range(5)] for r in range(5)]
    right = vadd(matvec(high_cols[:5], low_cols[5]), high_cols[5])
    from_high = resolve(factorize(system), right)
    from_low = vadd(matvec(low_cols[:5], from_high), low_cols[5])
    n_low = neighbour_value(from_low, low[30:], eps)
    n_high = neighbour_value([-e for e in from_high], high[30:], -eps)
    zero = jnp.zeros_like(n_low[0])
    as_low = [zero] * 5 + from_high + [zero] * 5 + n_high
    as_high = from_low + [zero] * 5 + n_low + [zero] * 5
    mine = [jnp.where(bit == 0, a, b) for a, b in zip(as_low, as_high)]
    values = [mine[5 * g : 5 * g + 5] for g in range(4)]
    descend(bits_ref[level - 1], face_ref, values, eps, own_out, partner_out)


def down_kernel(level, eps, planes, bits_ref, kept_ref, came_ref, face_ref, own_out, partner_out):
    bit = bits_ref[level + 1]
    mine = [join_halves(kept_ref[e], came_ref[e], bit, planes) for e in range(20)]
    values = [mine[5 * g : 5 * g + 5] for g in range(4)]
    descend(bits_ref[level], face_ref, values, eps, own_out, partner_out)


CELL = 8


def sweep_kernel(
    rows, half, bits_ref, state_ref, halo_ref, factor_ref, spike_ref, part_ref, keep_ref, send_ref,
    cell_ref, top_ref,
):
    planes = state_ref.shape[1] // rows
    lanes = state_ref.shape[2]
    diag, eps, scale = DIAGONAL / half, DAMPING / half, 1.0 / half
    lane = lax.broadcasted_iota(jnp.int32, (planes, lanes), 1)
    plane = lax.broadcasted_iota(jnp.int32, (planes, lanes), 0)

    def load_state(ref, i):
        return [ref[c, pl.ds(i, planes, stride=rows), :] for c in range(5)]

    def prepare(i, carry):
        fields = load_state(state_ref, i)
        cell = primitives(fields)
        u, v, w, kinetic, pressure, inverse = cell
        own = flux_along(fields, cell, 2)
        outer_fields = load_state(halo_ref, i)
        outer = flux_along(outer_fields, primitives(outer_fields), 2)
        normal = flux_along(fields, cell, 3)
        q = []
        for c in range(5):
            plus1 = pltpu.roll(jnp.where(lane < 1, outer[c], own[c]), lanes - 1, 1)
            plus2 = pltpu.roll(jnp.where(lane < 2, outer[c], own[c]), lanes - 2, 1)
            less1 = pltpu.roll(jnp.where(lane >= lanes - 1, outer[c], own[c]), 1, 1)
            less2 = pltpu.roll(jnp.where(lane >= lanes - 2, outer[c], own[c]), 2, 1)
            span = (less2 - plus2 + 8.0 * (plus1 - less1)) / 12.0
            mirror = normal[c] if c == 3 else -normal[c]
            below = jnp.where(plane == 0, mirror, pltpu.roll(normal[c], 1, 0))
            above = jnp.where(plane == planes - 1, normal[c], pltpu.roll(normal[c], planes - 1, 0))
            q.append(-span - 0.5 * (above - below))
        right = to_primitive(q, cell)
        right[0] = right[0] + fields[0]
        right[4] = right[4] + pressure
        for c in range(5):
            part_ref[5 * i + c] = right[c] * scale
        for c, value in enumerate((u, v, w, kinetic, pressure, GAMMA * pressure * inverse)):
            cell_ref[CELL * i + c] = value
        return carry

    lax.fori_loop(0, rows, prepare, 0)

    def cell_of(i):
        return [cell_ref[CELL * i + c] for c in range(6)]

    def store(ref, base, cols):
        for c in range(len(cols)):
            for r in range(5):
                value = cols[c][r]
                ref[base + 5 * c + r] = jnp.zeros((planes, lanes), jnp.float32) if value is None else value

    def load(ref, base, count):
        return [[ref[base + 5 * c + r] for r in range(5)] for c in range(count)]

    def first_row():
        here, after = cell_of(0), cell_of(1)
        inv = 1.0 / diag
        upper = upper_columns(differences(here, after), after[0] - eps, after[5])
        factor = [[mul(e, inv) for e in col] for col in upper]
        spike = [[mul(e, inv) for e in col] for col in primitive_columns(here)]
        part = [[e * inv for e in load(part_ref, 0, 1)[0]]]
        store(factor_ref, 0, factor)
        store(spike_ref, 0, spike)
        store(part_ref, 0, part)
        store(top_ref, 0, spike + factor + part)

    def row(i, final):
        before, here = cell_of(i - 1), cell_of(i)
        diff = differences(here, before)
        speed, sound = before[0] + eps, before[5]
        lower = lambda col: shift_frame(advect(col, speed, sound), diff)
        moved = [lower(col) for col in load(factor_ref, 25 * (i - 1), 5)]
        pivot = [[(diag - moved[c][r]) if r == c else -moved[c][r] for c in range(5)] for r in range(5)]
        factors = factorize(pivot)
        if final:
            upper = primitive_columns(here)
        else:
            after = cell_of(i + 1)
            upper = upper_columns(differences(here, after), after[0] - eps, after[5])
        factor = [resolve(factors, col) for col in upper]
        store(factor_ref, 25 * i, factor)
        spike = [resolve(factors, lower(col)) for col in load(spike_ref, 25 * (i - 1), 5)]
        store(spike_ref, 25 * i, spike)
        moved_part = lower(load(part_ref, 5 * (i - 1), 1)[0])
        part = resolve(factors, vadd(load(part_ref, 5 * i, 1)[0], moved_part))
        store(part_ref, 5 * i, [part])
        chain = load(top_ref, 25, 5)
        sums = [vadd(col, matvec(chain, new)) for col, new in zip(load(top_ref, 0, 5), spike)]
        const = vadd(load(top_ref, 50, 1)[0], matvec(chain, part))
        chain = [matvec(chain, col) for col in factor]
        store(top_ref, 0, sums + chain + [const])

    first_row()

    def inner(i, carry):
        row(i, False)
        return carry

    lax.fori_loop(1, rows - 1, inner, 0)
    row(rows - 1, True)

    end = rows - 1
    first_cell, last_cell = cell_of(0), cell_of(end)
    bottom = load(spike_ref, 25 * end, 5) + load(factor_ref, 25 * end, 5) + load(part_ref, 5 * end, 1)
    side1 = [
        to_conserved(advect(col, last_cell[0] + eps, last_cell[5]), last_cell) for col in bottom
    ]
    side0 = [
        [-e for e in to_conserved(advect(col, first_cell[0] - eps, first_cell[5]), first_cell)]
        for col in load(top_ref, 0, 11)
    ]
    emit_split(
        keep_ref, send_ref, bits_ref[0], (side0, side1),
        load_state(state_ref, 0), load_state(state_ref, end),
    )


def finish_kernel(
    rows, half, bits_ref, state_ref, factor_ref, spike_ref, part_ref, kept_ref, came_ref,
    next_ref, flux_ref,
):
    planes = state_ref.shape[1] // rows
    eps = DAMPING / half
    bit = bits_ref[0]
    mine = [join_halves(kept_ref[e], came_ref[e], bit, planes) for e in range(20)]
    low_in, high_in, low_n, high_n = (mine[5 * g : 5 * g + 5] for g in range(4))

    def load(ref, base, count):
        return [[ref[base + 5 * c + r] for r in range(5)] for c in range(count)]

    def step(k, carry):
        i = rows - 1 - k
        w, flux1, flux2 = carry
        spike, factor = load(spike_ref, 25 * i, 5), load(factor_ref, 25 * i, 5)
        part = load(part_ref, 5 * i, 1)[0]
        w = vadd(vadd(part, matvec(spike, low_in)), matvec(factor, w))
        fields = [state_ref[c, pl.ds(i, planes, stride=rows), :] for c in range(5)]
        u, v, speed_w, kinetic, pressure, inverse = primitives(fields)
        cell = (u, v, speed_w, kinetic)
        value = to_conserved(w, cell)
        flux0 = to_conserved(advect(w, u, GAMMA * pressure * inverse), cell)
        for c in range(5):
            next_ref[c, pl.ds(i, planes, stride=rows), :] = value[c]

        @pl.when(k > 0)
        def _():
            for c in range(5):
                flux_ref[c, pl.ds(i + 1, planes, stride=rows), :] = 0.5 * (flux0[c] - flux2[c])

        return w, flux0, flux1

    outer = [eps * n - g for n, g in zip(high_n, high_in)]
    zero = [jnp.zeros_like(e) for e in outer]
    _, flux1, flux2 = lax.fori_loop(0, rows, step, (high_in, outer, zero))
    inner = [g - eps * n for n, g in zip(low_n, low_in)]
    for c in range(5):
        flux_ref[c, pl.ds(0, planes, stride=rows), :] = 0.5 * (inner[c] - flux2[c])


def call(kernel, out_shapes, scratch=()):
    vmem = pl.BlockSpec(memory_space=pltpu.VMEM)

    def run(bits, *args):
        return pl.pallas_call(
            kernel,
            out_shape=[jax.ShapeDtypeStruct(s, jnp.float32) for s in out_shapes],
            in_specs=[pl.BlockSpec(memory_space=pltpu.SMEM)] + [vmem] * len(args),
            out_specs=[vmem] * len(out_shapes),
            scratch_shapes=[pltpu.VMEM(s, jnp.float32) for s in scratch],
        )(bits, *args)

    return run


def on_device(state):
    fields, planes, rows, lanes = state.shape
    half = 0.5 * 4.0 * rows
    eps = DAMPING / half
    size = lax.axis_size("stream")
    levels = size.bit_length() - 1
    place = lax.axis_index("stream")
    bits = jnp.stack([(place >> l) & 1 for l in range(levels)]).astype(jnp.int32)

    def swap(array, level):
        return lax.ppermute(array, "stream", [(s, s ^ (1 << level)) for s in range(size)])

    span = lax.axis_size("span")
    up = [(i, (i + 1) % span) for i in range(span)]
    left = lax.ppermute(state[..., -2:], "span", up)
    right = lax.ppermute(state[..., :2], "span", [(j, i) for i, j in up])
    halo = jnp.concatenate([right, state[..., 2:-2], left], axis=3)

    flat = (fields, planes * rows, lanes)
    tile = (planes, lanes)
    shapes = [tile]
    for _ in range(levels - 1):
        shapes.append(half_shape(shapes[-1]))
    state_rows = state.reshape(flat)
    factor, spike, part, own, sent = call(
        functools.partial(sweep_kernel, rows, half),
        [(25 * rows, *tile), (25 * rows, *tile), (5 * rows, *tile)] + [(PORT, *shapes[1])] * 2,
        [(CELL * rows, *tile), (SIDE, *tile)],
    )(bits, state_rows, halo.reshape(flat))
    faces = []
    for level in range(levels - 1):
        came = swap(sent, level)
        top = level == levels - 2
        out = (35, *shapes[level + 1]) if top else (PORT, *shapes[level + 2])
        own, sent, face = call(
            functools.partial(merge_kernel, level, top), [out, out, (PORT, *shapes[level + 1])]
        )(bits, own, came)
        faces.append(face)
    came = swap(sent, levels - 1)
    out = [(20, *shapes[levels - 1])] * 2
    own, sent = call(functools.partial(top_kernel, levels - 1, eps), out)(
        bits, own, came, faces[levels - 2]
    )
    for level in reversed(range(levels - 2)):
        came = swap(sent, level + 1)
        own, sent = call(
            functools.partial(down_kernel, level, eps, shapes[level + 1][0]),
            [(20, *shapes[level + 1])] * 2,
        )(bits, own, came, faces[level])
    came = swap(sent, 0)
    state_next, flux_difference = call(
        functools.partial(finish_kernel, rows, half), [flat, flat]
    )(bits, state_rows, factor, spike, part, own, came)
    return state_next.reshape(state.shape), flux_difference.reshape(state.shape)


def solution(mesh):
    spec = P(None, None, "stream", "span")
    return jax.shard_map(
        on_device, mesh=mesh, in_specs=(spec,), out_specs=(spec, spec), check_vma=False
    )
```

```python
import functools

import jax
import jax.numpy as jnp
from jax import lax
from jax.experimental import pallas as pl
from jax.experimental.pallas import tpu as pltpu
from jax.sharding import PartitionSpec as P

GAMMA = 1.4
GAMMA_LESS = 0.4
DAMPING = 0.125
DIAGONAL = 1.25

SIDE = 55
STATES = 110
PORT = 120


def add(a, b):
    return b if a is None else a if b is None else a + b


def sub(a, b):
    return a if b is None else -b if a is None else a - b


def mul(a, b):
    return None if a is None or b is None else a * b


def vadd(a, b):
    return [add(x, y) for x, y in zip(a, b)]


def matvec(cols, vec):
    out = []
    for row in range(5):
        acc = None
        for col in range(5):
            acc = add(acc, mul(cols[col][row], vec[col]))
        out.append(acc)
    return out


def factorize(rows):
    rows = [list(row) for row in rows]
    inverse = [None] * 5
    for k in range(5):
        inverse[k] = 1.0 / rows[k][k]
        for i in range(k + 1, 5):
            rows[i][k] = rows[i][k] * inverse[k]
            for j in range(k + 1, 5):
                rows[i][j] = sub(rows[i][j], mul(rows[i][k], rows[k][j]))
    return rows, inverse


def resolve(factors, vec):
    rows, inverse = factors
    x = list(vec)
    for i in range(5):
        for k in range(i):
            x[i] = sub(x[i], mul(rows[i][k], x[k]))
    for i in reversed(range(5)):
        for k in range(i + 1, 5):
            x[i] = sub(x[i], mul(rows[i][k], x[k]))
        x[i] = mul(x[i], inverse[i])
    return x


def primitives(fields):
    density, mom_x, mom_y, mom_z, energy = fields
    inverse = 1.0 / density
    u, v, w = mom_x * inverse, mom_y * inverse, mom_z * inverse
    kinetic = 0.5 * (u * u + v * v + w * w)
    pressure = GAMMA_LESS * (energy - density * kinetic)
    return u, v, w, kinetic, pressure, inverse


def differences(here, there):
    du, dv, dw = (b - a for a, b in zip(here[:3], there[:3]))
    half_square = 0.5 * GAMMA_LESS * (du * du + dv * dv + dw * dw)
    return du, dv, dw, half_square, GAMMA_LESS * du, GAMMA_LESS * dv, GAMMA_LESS * dw


def shift_frame(t, diff):
    du, dv, dw, half_square, du4, dv4, dw4 = diff
    return [
        t[0],
        t[1] + du * t[0],
        t[2] + dv * t[0],
        t[3] + dw * t[0],
        t[4] + half_square * t[0] + (du4 * t[1] + dv4 * t[2] + dw4 * t[3]),
    ]


def advect(x, speed, sound):
    return [
        speed * x[0] + x[1],
        speed * x[1] + x[4],
        speed * x[2],
        speed * x[3],
        speed * x[4] + sound * x[1],
    ]


def to_conserved(z, cell):
    u, v, w, kinetic = cell[:4]
    return [
        z[0],
        u * z[0] + z[1],
        v * z[0] + z[2],
        w * z[0] + z[3],
        kinetic * z[0] + u * z[1] + v * z[2] + w * z[3] + (1.0 / GAMMA_LESS) * z[4],
    ]


def to_primitive(x, cell):
    u, v, w, kinetic = cell[:4]
    return [
        x[0],
        x[1] - u * x[0],
        x[2] - v * x[0],
        x[3] - w * x[0],
        GAMMA_LESS * (kinetic * x[0] - u * x[1] - v * x[2] - w * x[3] + x[4]),
    ]


def primitive_columns(cell):
    u, v, w, kinetic = cell[:4]
    one = jnp.ones_like(u)
    return [
        [one, -u, -v, -w, GAMMA_LESS * kinetic],
        [None, one, None, None, -GAMMA_LESS * u],
        [None, None, one, None, -GAMMA_LESS * v],
        [None, None, None, one, -GAMMA_LESS * w],
        [None, None, None, None, GAMMA_LESS * one],
    ]


def upper_columns(diff, speed, sound):
    du, dv, dw, half_square, du4, dv4, dw4 = diff
    less = -speed
    one = jnp.ones_like(speed)
    return [
        [less, du * less, dv * less, dw * less, half_square * less],
        [-one, -(du + speed), -dv, -dw, du4 * less - (half_square + sound)],
        [None, None, less, None, dv4 * less],
        [None, None, None, less, dw4 * less],
        [None, -one, None, None, -(du4 + speed)],
    ]


def neighbour_value(coupling, fields, eps):
    u, v, w, kinetic, pressure, inverse = primitives(fields)
    z = to_primitive(coupling, (u, v, w, kinetic))
    speed = u + eps
    sound = GAMMA * pressure * inverse
    over = 1.0 / speed
    det = 1.0 / (speed * speed - sound)
    w1 = (speed * z[1] - z[4]) * det
    w4 = (speed * z[4] - sound * z[1]) * det
    return to_conserved([(z[0] - w1) * over, w1, z[2] * over, z[3] * over, w4], (u, v, w, kinetic))


def flux_along(fields, cell, direction):
    pressure = cell[4]
    normal = cell[direction - 1]
    columns = [normal * fields[m] for m in range(4)]
    columns.append(normal * (fields[4] + pressure))
    columns[direction] = columns[direction] + pressure
    return columns


def merge(low, high):
    a1, a2 = low
    b1, b2 = high
    product = [matvec(b1[:5], col) for col in a2[5:10]]
    one = jnp.ones_like(product[0][0])
    system = [[(one if r == c else 0.0) - product[c][r] for c in range(5)] for r in range(5)]
    factors = factorize(system)
    columns = [matvec(b1[:5], col) for col in a2[:5]] + b1[5:10]
    columns.append(vadd(matvec(b1[:5], a2[10]), b1[10]))
    down = [resolve(factors, col) for col in columns]
    up = [matvec(a2[5:10], col) for col in down]
    up = [vadd(up[c], a2[c]) for c in range(5)] + up[5:10] + [vadd(up[10], a2[10])]
    out1 = [matvec(a1[5:10], col) for col in down]
    out1 = [vadd(out1[c], a1[c]) for c in range(5)] + out1[5:10] + [vadd(out1[10], a1[10])]
    out2 = [matvec(b2[:5], col) for col in up]
    out2 = out2[:5] + [vadd(out2[c], b2[c]) for c in range(5, 10)] + [vadd(out2[10], b2[10])]
    return (out1, out2), down, up


def split_halves(value, bit):
    planes, lanes = value.shape
    if planes > 1:
        halves = value[: planes // 2], value[planes // 2 :]
    else:
        halves = value[:, : lanes // 2], value[:, lanes // 2 :]
    return jnp.where(bit == 0, halves[0], halves[1]), jnp.where(bit == 0, halves[1], halves[0])


def join_halves(kept, came, bit, planes):
    axis = 0 if planes > 1 else 1
    low = jnp.where(bit == 0, kept, came)
    high = jnp.where(bit == 0, came, kept)
    return jnp.concatenate([low, high], axis=axis)


def half_shape(shape):
    planes, lanes = shape
    return (planes // 2, lanes) if planes > 1 else (planes, lanes // 2)


def unpack_port(load):
    sides = [[[load(s * SIDE + 5 * c + r) for r in range(5)] for c in range(11)] for s in range(2)]
    first = [load(STATES + r) for r in range(5)]
    last = [load(STATES + 5 + r) for r in range(5)]
    return sides, first, last


def emit_split(keep_ref, send_ref, bit, sides, first, last):
    def emit(index, value):
        kept, sent = split_halves(value, bit)
        keep_ref[index] = kept
        send_ref[index] = sent

    for s in range(2):
        for c in range(11):
            for r in range(5):
                emit(s * SIDE + 5 * c + r, sides[s][c][r])
    for r in range(5):
        emit(STATES + r, first[r])
        emit(STATES + 5 + r, last[r])


def emit_facing(keep_ref, send_ref, bit, sides, first, last):
    for c in range(6):
        for r in range(5):
            as_low = sides[1][5 + c][r]
            as_high = sides[0][c if c < 5 else 10][r]
            value = jnp.where(bit == 0, as_low, as_high)
            keep_ref[5 * c + r] = value
            send_ref[5 * c + r] = value
    for r in range(5):
        value = jnp.where(bit == 0, last[r], first[r])
        keep_ref[30 + r] = value
        send_ref[30 + r] = value


def merge_kernel(level, top, bits_ref, own_ref, came_ref, keep_ref, send_ref, face_ref):
    bit = bits_ref[level]
    low = lambda e: jnp.where(bit == 0, own_ref[e], came_ref[e])
    high = lambda e: jnp.where(bit == 0, came_ref[e], own_ref[e])
    low_sides, first, low_last = unpack_port(low)
    high_sides, high_first, last = unpack_port(high)
    sides, down, up = merge(low_sides, high_sides)
    for c in range(11):
        for r in range(5):
            face_ref[5 * c + r] = down[c][r]
            face_ref[SIDE + 5 * c + r] = up[c][r]
    for r in range(5):
        face_ref[STATES + r] = low_last[r]
        face_ref[STATES + 5 + r] = high_first[r]
    emit = emit_facing if top else emit_split
    emit(keep_ref, send_ref, bits_ref[level + 1], sides, first, last)


def descend(bit, face_ref, values, eps, own_ref, partner_ref):
    low_in, high_in, low_n, high_n = values
    down, up = (
        [[face_ref[s * SIDE + 5 * c + r] for r in range(5)] for c in range(11)] for s in range(2)
    )
    from_high = vadd(vadd(matvec(down[:5], low_in), matvec(down[5:10], high_in)), down[10])
    from_low = vadd(vadd(matvec(up[:5], low_in), matvec(up[5:10], high_in)), up[10])
    low_last = [face_ref[STATES + r] for r in range(5)]
    high_first = [face_ref[STATES + 5 + r] for r in range(5)]
    n_low = neighbour_value(from_low, low_last, eps)
    n_high = neighbour_value([-e for e in from_high], high_first, -eps)
    as_low = low_in + from_high + low_n + n_high
    as_high = from_low + high_in + n_low + high_n
    for e in range(20):
        own_ref[e] = jnp.where(bit == 0, as_low[e], as_high[e])
        partner_ref[e] = jnp.where(bit == 0, as_high[e], as_low[e])


def top_kernel(level, eps, bits_ref, own_ref, came_ref, face_ref, own_out, partner_out):
    bit = bits_ref[level]
    low = [jnp.where(bit == 0, own_ref[e], came_ref[e]) for e in range(35)]
    high = [jnp.where(bit == 0, came_ref[e], own_ref[e]) for e in range(35)]
    low_cols = [low[5 * c : 5 * c + 5] for c in range(6)]
    high_cols = [high[5 * c : 5 * c + 5] for c in range(6)]
    product = [matvec(high_cols[:5], col) for col in low_cols[:5]]
    system = [[(1.0 if r == c else 0.0) - product[c][r] for c in range(5)] for r in range(5)]
    right = vadd(matvec(high_cols[:5], low_cols[5]), high_cols[5])
    from_high = resolve(factorize(system), right)
    from_low = vadd(matvec(low_cols[:5], from_high), low_cols[5])
    n_low = neighbour_value(from_low, low[30:], eps)
    n_high = neighbour_value([-e for e in from_high], high[30:], -eps)
    zero = jnp.zeros_like(n_low[0])
    as_low = [zero] * 5 + from_high + [zero] * 5 + n_high
    as_high = from_low + [zero] * 5 + n_low + [zero] * 5
    mine = [jnp.where(bit == 0, a, b) for a, b in zip(as_low, as_high)]
    values = [mine[5 * g : 5 * g + 5] for g in range(4)]
    descend(bits_ref[level - 1], face_ref, values, eps, own_out, partner_out)


def down_kernel(level, eps, planes, bits_ref, kept_ref, came_ref, face_ref, own_out, partner_out):
    bit = bits_ref[level + 1]
    mine = [join_halves(kept_ref[e], came_ref[e], bit, planes) for e in range(20)]
    values = [mine[5 * g : 5 * g + 5] for g in range(4)]
    descend(bits_ref[level], face_ref, values, eps, own_out, partner_out)


CELL = 8


def sweep_kernel(
    rows, half, bits_ref, state_ref, halo_ref, factor_ref, spike_ref, part_ref, keep_ref, send_ref,
    cell_ref, top_ref,
):
    planes = state_ref.shape[1] // rows
    lanes = state_ref.shape[2]
    diag, eps, scale = DIAGONAL / half, DAMPING / half, 1.0 / half
    lane = lax.broadcasted_iota(jnp.int32, (planes, lanes), 1)
    plane = lax.broadcasted_iota(jnp.int32, (planes, lanes), 0)

    def load_state(ref, i):
        return [ref[c, pl.ds(i, planes, stride=rows), :] for c in range(5)]

    def prepare(i, carry):
        fields = load_state(state_ref, i)
        cell = primitives(fields)
        u, v, w, kinetic, pressure, inverse = cell
        own = flux_along(fields, cell, 2)
        outer_fields = load_state(halo_ref, i)
        outer = flux_along(outer_fields, primitives(outer_fields), 2)
        normal = flux_along(fields, cell, 3)
        q = []
        for c in range(5):
            plus1 = pltpu.roll(jnp.where(lane < 1, outer[c], own[c]), lanes - 1, 1)
            plus2 = pltpu.roll(jnp.where(lane < 2, outer[c], own[c]), lanes - 2, 1)
            less1 = pltpu.roll(jnp.where(lane >= lanes - 1, outer[c], own[c]), 1, 1)
            less2 = pltpu.roll(jnp.where(lane >= lanes - 2, outer[c], own[c]), 2, 1)
            span = (less2 - plus2 + 8.0 * (plus1 - less1)) / 12.0
            mirror = normal[c] if c == 3 else -normal[c]
            below = jnp.where(plane == 0, mirror, pltpu.roll(normal[c], 1, 0))
            above = jnp.where(plane == planes - 1, normal[c], pltpu.roll(normal[c], planes - 1, 0))
            q.append(-span - 0.5 * (above - below))
        right = to_primitive(q, cell)
        right[0] = right[0] + fields[0]
        right[4] = right[4] + pressure
        for c in range(5):
            part_ref[5 * i + c] = right[c] * scale
        for c, value in enumerate((u, v, w, kinetic, pressure, GAMMA * pressure * inverse)):
            cell_ref[CELL * i + c] = value
        return carry

    lax.fori_loop(0, rows, prepare, 0)

    def cell_of(i):
        return [cell_ref[CELL * i + c] for c in range(6)]

    def store(ref, base, cols):
        for c in range(len(cols)):
            for r in range(5):
                value = cols[c][r]
                ref[base + 5 * c + r] = jnp.zeros((planes, lanes), jnp.float32) if value is None else value

    def load(ref, base, count):
        return [[ref[base + 5 * c + r] for r in range(5)] for c in range(count)]

    def first_row():
        here, after = cell_of(0), cell_of(1)
        inv = 1.0 / diag
        upper = upper_columns(differences(here, after), after[0] - eps, after[5])
        factor = [[mul(e, inv) for e in col] for col in upper]
        spike = [[mul(e, inv) for e in col] for col in primitive_columns(here)]
        part = [[e * inv for e in load(part_ref, 0, 1)[0]]]
        store(factor_ref, 0, factor)
        store(spike_ref, 0, spike)
        store(part_ref, 0, part)
        store(top_ref, 0, spike + factor + part)

    def row(i, final):
        before, here = cell_of(i - 1), cell_of(i)
        diff = differences(here, before)
        speed, sound = before[0] + eps, before[5]
        lower = lambda col: shift_frame(advect(col, speed, sound), diff)
        moved = [lower(col) for col in load(factor_ref, 25 * (i - 1), 5)]
        pivot = [[(diag - moved[c][r]) if r == c else -moved[c][r] for c in range(5)] for r in range(5)]
        factors = factorize(pivot)
        if final:
            upper = primitive_columns(here)
        else:
            after = cell_of(i + 1)
            upper = upper_columns(differences(here, after), after[0] - eps, after[5])
        factor = [resolve(factors, col) for col in upper]
        store(factor_ref, 25 * i, factor)
        spike = [resolve(factors, lower(col)) for col in load(spike_ref, 25 * (i - 1), 5)]
        store(spike_ref, 25 * i, spike)
        moved_part = lower(load(part_ref, 5 * (i - 1), 1)[0])
        part = resolve(factors, vadd(load(part_ref, 5 * i, 1)[0], moved_part))
        store(part_ref, 5 * i, [part])
        chain = load(top_ref, 25, 5)
        sums = [vadd(col, matvec(chain, new)) for col, new in zip(load(top_ref, 0, 5), spike)]
        const = vadd(load(top_ref, 50, 1)[0], matvec(chain, part))
        chain = [matvec(chain, col) for col in factor]
        store(top_ref, 0, sums + chain + [const])

    first_row()

    def inner(i, carry):
        row(i, False)
        return carry

    lax.fori_loop(1, rows - 1, inner, 0)
    row(rows - 1, True)

    end = rows - 1
    first_cell, last_cell = cell_of(0), cell_of(end)
    bottom = load(spike_ref, 25 * end, 5) + load(factor_ref, 25 * end, 5) + load(part_ref, 5 * end, 1)
    side1 = [
        to_conserved(advect(col, last_cell[0] + eps, last_cell[5]), last_cell) for col in bottom
    ]
    side0 = [
        [-e for e in to_conserved(advect(col, first_cell[0] - eps, first_cell[5]), first_cell)]
        for col in load(top_ref, 0, 11)
    ]
    emit_split(
        keep_ref, send_ref, bits_ref[0], (side0, side1),
        load_state(state_ref, 0), load_state(state_ref, end),
    )


def finish_kernel(
    rows, half, bits_ref, state_ref, factor_ref, spike_ref, part_ref, kept_ref, came_ref,
    next_ref, flux_ref,
):
    planes = state_ref.shape[1] // rows
    eps = DAMPING / half
    bit = bits_ref[0]
    mine = [join_halves(kept_ref[e], came_ref[e], bit, planes) for e in range(20)]
    low_in, high_in, low_n, high_n = (mine[5 * g : 5 * g + 5] for g in range(4))

    def load(ref, base, count):
        return [[ref[base + 5 * c + r] for r in range(5)] for c in range(count)]

    def step(k, carry):
        i = rows - 1 - k
        w, flux1, flux2 = carry
        spike, factor = load(spike_ref, 25 * i, 5), load(factor_ref, 25 * i, 5)
        part = load(part_ref, 5 * i, 1)[0]
        w = vadd(vadd(part, matvec(spike, low_in)), matvec(factor, w))
        fields = [state_ref[c, pl.ds(i, planes, stride=rows), :] for c in range(5)]
        u, v, speed_w, kinetic, pressure, inverse = primitives(fields)
        cell = (u, v, speed_w, kinetic)
        value = to_conserved(w, cell)
        flux0 = to_conserved(advect(w, u, GAMMA * pressure * inverse), cell)
        for c in range(5):
            next_ref[c, pl.ds(i, planes, stride=rows), :] = value[c]

        @pl.when(k > 0)
        def _():
            for c in range(5):
                flux_ref[c, pl.ds(i + 1, planes, stride=rows), :] = 0.5 * (flux0[c] - flux2[c])

        return w, flux0, flux1

    outer = [eps * n - g for n, g in zip(high_n, high_in)]
    zero = [jnp.zeros_like(e) for e in outer]
    _, flux1, flux2 = lax.fori_loop(0, rows, step, (high_in, outer, zero))
    inner = [g - eps * n for n, g in zip(low_n, low_in)]
    for c in range(5):
        flux_ref[c, pl.ds(0, planes, stride=rows), :] = 0.5 * (inner[c] - flux2[c])


def call(kernel, out_shapes, scratch=()):
    vmem = pl.BlockSpec(memory_space=pltpu.VMEM)

    def run(bits, *args):
        return pl.pallas_call(
            kernel,
            out_shape=[jax.ShapeDtypeStruct(s, jnp.float32) for s in out_shapes],
            in_specs=[pl.BlockSpec(memory_space=pltpu.SMEM)] + [vmem] * len(args),
            out_specs=[vmem] * len(out_shapes),
            compiler_params=pltpu.CompilerParams(vmem_limit_bytes=16 << 20),
            scratch_shapes=[pltpu.VMEM(s, jnp.float32) for s in scratch],
        )(bits, *args)

    return run


def on_device(state):
    fields, planes, rows, lanes = state.shape
    half = 0.5 * 4.0 * rows
    eps = DAMPING / half
    size = lax.axis_size("stream")
    levels = size.bit_length() - 1
    place = lax.axis_index("stream")
    bits = jnp.stack([(place >> l) & 1 for l in range(levels)]).astype(jnp.int32)

    def swap(array, level):
        return lax.ppermute(array, "stream", [(s, s ^ (1 << level)) for s in range(size)])

    span = lax.axis_size("span")
    up = [(i, (i + 1) % span) for i in range(span)]
    left = lax.ppermute(state[..., -2:], "span", up)
    right = lax.ppermute(state[..., :2], "span", [(j, i) for i, j in up])
    halo = jnp.concatenate([right, state[..., 2:-2], left], axis=3)

    flat = (fields, planes * rows, lanes)
    tile = (planes, lanes)
    shapes = [tile]
    for _ in range(levels - 1):
        shapes.append(half_shape(shapes[-1]))
    state_rows = state.reshape(flat)
    factor, spike, part, own, sent = call(
        functools.partial(sweep_kernel, rows, half),
        [(25 * rows, *tile), (25 * rows, *tile), (5 * rows, *tile)] + [(PORT, *shapes[1])] * 2,
        [(CELL * rows, *tile), (SIDE, *tile)],
    )(bits, state_rows, halo.reshape(flat))
    faces = []
    for level in range(levels - 1):
        came = swap(sent, level)
        top = level == levels - 2
        out = (35, *shapes[level + 1]) if top else (PORT, *shapes[level + 2])
        own, sent, face = call(
            functools.partial(merge_kernel, level, top), [out, out, (PORT, *shapes[level + 1])]
        )(bits, own, came)
        faces.append(face)
    came = swap(sent, levels - 1)
    out = [(20, *shapes[levels - 1])] * 2
    own, sent = call(functools.partial(top_kernel, levels - 1, eps), out)(
        bits, own, came, faces[levels - 2]
    )
    for level in reversed(range(levels - 2)):
        came = swap(sent, level + 1)
        own, sent = call(
            functools.partial(down_kernel, level, eps, shapes[level + 1][0]),
            [(20, *shapes[level + 1])] * 2,
        )(bits, own, came, faces[level])
    came = swap(sent, 0)
    state_next, flux_difference = call(
        functools.partial(finish_kernel, rows, half), [flat, flat]
    )(bits, state_rows, factor, spike, part, own, came)
    return state_next.reshape(state.shape), flux_difference.reshape(state.shape)


def solution(mesh):
    spec = P(None, None, "stream", "span")
    return jax.shard_map(
        on_device, mesh=mesh, in_specs=(spec,), out_specs=(spec, spec), check_vma=False
    )
```

```python
import functools

import jax
import jax.numpy as jnp
from jax import lax
from jax.experimental import pallas as pl
from jax.experimental.pallas import tpu as pltpu
from jax.sharding import PartitionSpec as P

GAMMA = 1.4
GAMMA_LESS = 0.4
DAMPING = 0.125
DIAGONAL = 1.25

MATRIX = 50
VECTOR = 20
PORT = 2 * MATRIX + VECTOR
SIDE = 55
STATES = 110


def add(a, b):
    return b if a is None else a if b is None else a + b


def sub(a, b):
    return a if b is None else -b if a is None else a - b


def mul(a, b):
    return None if a is None or b is None else a * b


def vadd(a, b):
    return [add(x, y) for x, y in zip(a, b)]


def matvec(cols, vec):
    out = []
    for row in range(5):
        acc = None
        for col in range(5):
            acc = add(acc, mul(cols[col][row], vec[col]))
        out.append(acc)
    return out


def factorize(rows):
    rows = [list(row) for row in rows]
    inverse = [None] * 5
    for k in range(5):
        inverse[k] = 1.0 / rows[k][k]
        for i in range(k + 1, 5):
            rows[i][k] = rows[i][k] * inverse[k]
            for j in range(k + 1, 5):
                rows[i][j] = sub(rows[i][j], mul(rows[i][k], rows[k][j]))
    return rows, inverse


def resolve(factors, vec):
    rows, inverse = factors
    x = list(vec)
    for i in range(5):
        for k in range(i):
            x[i] = sub(x[i], mul(rows[i][k], x[k]))
    for i in reversed(range(5)):
        for k in range(i + 1, 5):
            x[i] = sub(x[i], mul(rows[i][k], x[k]))
        x[i] = mul(x[i], inverse[i])
    return x


def primitives(fields):
    density, mom_x, mom_y, mom_z, energy = fields
    inverse = 1.0 / density
    u, v, w = mom_x * inverse, mom_y * inverse, mom_z * inverse
    kinetic = 0.5 * (u * u + v * v + w * w)
    pressure = GAMMA_LESS * (energy - density * kinetic)
    return u, v, w, kinetic, pressure, inverse


def differences(here, there):
    du, dv, dw = (b - a for a, b in zip(here[:3], there[:3]))
    half_square = 0.5 * GAMMA_LESS * (du * du + dv * dv + dw * dw)
    return du, dv, dw, half_square, GAMMA_LESS * du, GAMMA_LESS * dv, GAMMA_LESS * dw


def shift_frame(t, diff):
    du, dv, dw, half_square, du4, dv4, dw4 = diff
    return [
        t[0],
        t[1] + du * t[0],
        t[2] + dv * t[0],
        t[3] + dw * t[0],
        t[4] + half_square * t[0] + (du4 * t[1] + dv4 * t[2] + dw4 * t[3]),
    ]


def advect(x, speed, sound):
    return [
        speed * x[0] + x[1],
        speed * x[1] + x[4],
        speed * x[2],
        speed * x[3],
        speed * x[4] + sound * x[1],
    ]


def to_conserved(z, cell):
    u, v, w, kinetic = cell[:4]
    return [
        z[0],
        u * z[0] + z[1],
        v * z[0] + z[2],
        w * z[0] + z[3],
        kinetic * z[0] + u * z[1] + v * z[2] + w * z[3] + (1.0 / GAMMA_LESS) * z[4],
    ]


def to_primitive(x, cell):
    u, v, w, kinetic = cell[:4]
    return [
        x[0],
        x[1] - u * x[0],
        x[2] - v * x[0],
        x[3] - w * x[0],
        GAMMA_LESS * (kinetic * x[0] - u * x[1] - v * x[2] - w * x[3] + x[4]),
    ]


def primitive_columns(cell):
    u, v, w, kinetic = cell[:4]
    one = jnp.ones_like(u)
    return [
        [one, -u, -v, -w, GAMMA_LESS * kinetic],
        [None, one, None, None, -GAMMA_LESS * u],
        [None, None, one, None, -GAMMA_LESS * v],
        [None, None, None, one, -GAMMA_LESS * w],
        [None, None, None, None, GAMMA_LESS * one],
    ]


def upper_columns(diff, speed, sound):
    du, dv, dw, half_square, du4, dv4, dw4 = diff
    less = -speed
    one = jnp.ones_like(speed)
    return [
        [less, du * less, dv * less, dw * less, half_square * less],
        [-one, -(du + speed), -dv, -dw, du4 * less - (half_square + sound)],
        [None, None, less, None, dv4 * less],
        [None, None, None, less, dw4 * less],
        [None, -one, None, None, -(du4 + speed)],
    ]


def neighbour_value(coupling, fields, eps):
    u, v, w, kinetic, pressure, inverse = primitives(fields)
    z = to_primitive(coupling, (u, v, w, kinetic))
    speed = u + eps
    sound = GAMMA * pressure * inverse
    over = 1.0 / speed
    det = 1.0 / (speed * speed - sound)
    w1 = (speed * z[1] - z[4]) * det
    w4 = (speed * z[4] - sound * z[1]) * det
    return to_conserved([(z[0] - w1) * over, w1, z[2] * over, z[3] * over, w4], (u, v, w, kinetic))


def flux_along(fields, cell, direction):
    pressure = cell[4]
    normal = cell[direction - 1]
    columns = [normal * fields[m] for m in range(4)]
    columns.append(normal * (fields[4] + pressure))
    columns[direction] = columns[direction] + pressure
    return columns


def merge(low, high):
    a1, a2 = low
    b1, b2 = high
    product = [matvec(b1[:5], col) for col in a2[5:10]]
    one = jnp.ones_like(product[0][0])
    system = [[(one if r == c else 0.0) - product[c][r] for c in range(5)] for r in range(5)]
    factors = factorize(system)
    columns = [matvec(b1[:5], col) for col in a2[:5]] + b1[5:10]
    columns.append(vadd(matvec(b1[:5], a2[10]), b1[10]))
    down = [resolve(factors, col) for col in columns]
    up = [matvec(a2[5:10], col) for col in down]
    up = [vadd(up[c], a2[c]) for c in range(5)] + up[5:10] + [vadd(up[10], a2[10])]
    out1 = [matvec(a1[5:10], col) for col in down]
    out1 = [vadd(out1[c], a1[c]) for c in range(5)] + out1[5:10] + [vadd(out1[10], a1[10])]
    out2 = [matvec(b2[:5], col) for col in up]
    out2 = out2[:5] + [vadd(out2[c], b2[c]) for c in range(5, 10)] + [vadd(out2[10], b2[10])]
    return (out1, out2), down, up


def split_halves(value, bit):
    planes, lanes = value.shape
    if planes > 1:
        halves = value[: planes // 2], value[planes // 2 :]
    else:
        halves = value[:, : lanes // 2], value[:, lanes // 2 :]
    return jnp.where(bit == 0, halves[0], halves[1]), jnp.where(bit == 0, halves[1], halves[0])


def join_halves(kept, came, bit, planes):
    axis = 0 if planes > 1 else 1
    low = jnp.where(bit == 0, kept, came)
    high = jnp.where(bit == 0, came, kept)
    return jnp.concatenate([low, high], axis=axis)


def half_shape(shape):
    planes, lanes = shape
    return (planes // 2, lanes) if planes > 1 else (planes, lanes // 2)


def unpack_port(load):
    sides = []
    for s in range(2):
        cols = [[load(MATRIX * s + 5 * c + r) for r in range(5)] for c in range(10)]
        sides.append(cols + [[load(2 * MATRIX + 5 * s + r) for r in range(5)]])
    first = [load(2 * MATRIX + 10 + r) for r in range(5)]
    last = [load(2 * MATRIX + 15 + r) for r in range(5)]
    return sides, first, last


def emit_list(keep_ref, send_ref, bit, values, base=0):
    for e, value in enumerate(values):
        kept, sent = split_halves(value, bit)
        keep_ref[base + e] = kept
        send_ref[base + e] = sent


def flatten(cols):
    return [value for col in cols for value in col]


def emit_split(keep_ref, send_ref, bit, sides, first, last):
    values = flatten(sides[0][:10] + sides[1][:10] + [sides[0][10], sides[1][10], first, last])
    emit_list(keep_ref, send_ref, bit, values)


def emit_facing(keep_ref, send_ref, bit, sides, first, last):
    for c in range(6):
        for r in range(5):
            as_low = sides[1][5 + c][r]
            as_high = sides[0][c if c < 5 else 10][r]
            value = jnp.where(bit == 0, as_low, as_high)
            keep_ref[5 * c + r] = value
            send_ref[5 * c + r] = value
    for r in range(5):
        value = jnp.where(bit == 0, last[r], first[r])
        keep_ref[30 + r] = value
        send_ref[30 + r] = value


def piecewise(refs, sizes):
    def load(e):
        for ref, size in zip(refs, sizes):
            if e < size:
                return ref[e]
            e -= size

    return load


def merge_kernel(level, top, sizes, bits_ref, *refs):
    count = len(sizes)
    own, came = piecewise(refs[:count], sizes), piecewise(refs[count : 2 * count], sizes)
    keep_ref, send_ref, face_ref = refs[2 * count :]
    bit = bits_ref[level]
    low = lambda e: jnp.where(bit == 0, own(e), came(e))
    high = lambda e: jnp.where(bit == 0, came(e), own(e))
    low_sides, first, low_last = unpack_port(low)
    high_sides, high_first, last = unpack_port(high)
    sides, down, up = merge(low_sides, high_sides)
    for c in range(11):
        for r in range(5):
            face_ref[5 * c + r] = down[c][r]
            face_ref[SIDE + 5 * c + r] = up[c][r]
    for r in range(5):
        face_ref[STATES + r] = low_last[r]
        face_ref[STATES + 5 + r] = high_first[r]
    emit = emit_facing if top else emit_split
    emit(keep_ref, send_ref, bits_ref[level + 1], sides, first, last)


def descend(bit, face_ref, values, eps, own_ref, partner_ref):
    low_in, high_in, low_n, high_n = values
    down, up = (
        [[face_ref[s * SIDE + 5 * c + r] for r in range(5)] for c in range(11)] for s in range(2)
    )
    from_high = vadd(vadd(matvec(down[:5], low_in), matvec(down[5:10], high_in)), down[10])
    from_low = vadd(vadd(matvec(up[:5], low_in), matvec(up[5:10], high_in)), up[10])
    low_last = [face_ref[STATES + r] for r in range(5)]
    high_first = [face_ref[STATES + 5 + r] for r in range(5)]
    n_low = neighbour_value(from_low, low_last, eps)
    n_high = neighbour_value([-e for e in from_high], high_first, -eps)
    as_low = low_in + from_high + low_n + n_high
    as_high = from_low + high_in + n_low + high_n
    for e in range(20):
        own_ref[e] = jnp.where(bit == 0, as_low[e], as_high[e])
        partner_ref[e] = jnp.where(bit == 0, as_high[e], as_low[e])


def top_kernel(level, eps, bits_ref, own_ref, came_ref, face_ref, own_out, partner_out):
    bit = bits_ref[level]
    low = [jnp.where(bit == 0, own_ref[e], came_ref[e]) for e in range(35)]
    high = [jnp.where(bit == 0, came_ref[e], own_ref[e]) for e in range(35)]
    low_cols = [low[5 * c : 5 * c + 5] for c in range(6)]
    high_cols = [high[5 * c : 5 * c + 5] for c in range(6)]
    product = [matvec(high_cols[:5], col) for col in low_cols[:5]]
    system = [[(1.0 if r == c else 0.0) - product[c][r] for c in range(5)] for r in range(5)]
    right = vadd(matvec(high_cols[:5], low_cols[5]), high_cols[5])
    from_high = resolve(factorize(system), right)
    from_low = vadd(matvec(low_cols[:5], from_high), low_cols[5])
    n_low = neighbour_value(from_low, low[30:], eps)
    n_high = neighbour_value([-e for e in from_high], high[30:], -eps)
    zero = jnp.zeros_like(n_low[0])
    as_low = [zero] * 5 + from_high + [zero] * 5 + n_high
    as_high = from_low + [zero] * 5 + n_low + [zero] * 5
    mine = [jnp.where(bit == 0, a, b) for a, b in zip(as_low, as_high)]
    values = [mine[5 * g : 5 * g + 5] for g in range(4)]
    descend(bits_ref[level - 1], face_ref, values, eps, own_out, partner_out)


def down_kernel(level, eps, planes, bits_ref, kept_ref, came_ref, face_ref, own_out, partner_out):
    bit = bits_ref[level + 1]
    mine = [join_halves(kept_ref[e], came_ref[e], bit, planes) for e in range(20)]
    values = [mine[5 * g : 5 * g + 5] for g in range(4)]
    descend(bits_ref[level], face_ref, values, eps, own_out, partner_out)


CELL = 6
EDGE = 2


def load_columns(ref, base, count):
    return [[ref[base + 5 * c + r] for r in range(5)] for c in range(count)]


def store_columns(ref, base, cols):
    for c in range(len(cols)):
        for r in range(5):
            value = cols[c][r]
            ref[base + 5 * c + r] = jnp.zeros(ref.shape[1:], ref.dtype) if value is None else value


def load_cell(ref, i):
    return [ref[CELL * i + c] for c in range(CELL)]


def load_state(ref, i, planes, rows):
    return [ref[c, pl.ds(i, planes, stride=rows), :] for c in range(5)]


def edge_selector(lanes):
    row = lax.broadcasted_iota(jnp.int32, (8, lanes), 0)
    lane = lax.broadcasted_iota(jnp.int32, (8, lanes), 1)
    target = jnp.where(row < EDGE, row, lanes - 2 * EDGE + row)
    return jnp.where((row < 2 * EDGE) & (lane == target), 1.0, 0.0).astype(jnp.float32)


def sweep_kernel(
    rows, half, bits_ref, state_ref, factor_ref, spike_ref, lu_ref, cell_ref, head_ref, tail_ref,
    keep_ref, send_ref,
):
    planes = state_ref.shape[1] // rows
    lanes = state_ref.shape[2]
    diag, eps = DIAGONAL / half, DAMPING / half
    selector = edge_selector(lanes)
    for c in range(5):
        edges = lax.dot_general(
            selector, state_ref[c], (((1,), (1,)), ((), ())),
            precision=lax.Precision.HIGHEST, preferred_element_type=jnp.float32,
        )
        head_ref[c] = edges[:EDGE]
        tail_ref[c] = edges[EDGE : 2 * EDGE]

    def prepare(i):
        u, v, w, kinetic, pressure, inverse = primitives(load_state(state_ref, i, planes, rows))
        cell = (u, v, w, kinetic, pressure, GAMMA * pressure * inverse)
        for c, value in enumerate(cell):
            cell_ref[CELL * i + c] = value
        return cell

    here, after = prepare(0), prepare(1)
    inv = 1.0 / diag
    upper = upper_columns(differences(here, after), after[0] - eps, after[5])
    store_columns(factor_ref, 0, [[mul(e, inv) for e in col] for col in upper])
    store_columns(spike_ref, 0, [[mul(e, inv) for e in col] for col in primitive_columns(here)])

    def row(i, final):
        before, here = load_cell(cell_ref, i - 1), load_cell(cell_ref, i)
        diff = differences(here, before)
        speed, sound = before[0] + eps, before[5]
        lower = lambda col: shift_frame(advect(col, speed, sound), diff)
        moved = [lower(col) for col in load_columns(factor_ref, 25 * (i - 1), 5)]
        pivot = [[(diag - moved[c][r]) if r == c else -moved[c][r] for c in range(5)] for r in range(5)]
        factors = factorize(pivot)
        for r in range(5):
            for c in range(5):
                lu_ref[25 * i + 5 * r + c] = factors[1][r] if r == c else factors[0][r][c]
        if final:
            upper = primitive_columns(here)
        else:
            after = prepare(i + 1)
            upper = upper_columns(differences(here, after), after[0] - eps, after[5])
        store_columns(factor_ref, 25 * i, [resolve(factors, col) for col in upper])
        spike = [resolve(factors, lower(col)) for col in load_columns(spike_ref, 25 * (i - 1), 5)]
        store_columns(spike_ref, 25 * i, spike)

    def inner(i, carry):
        row(i, False)
        return carry

    lax.fori_loop(1, rows - 1, inner, 0)
    end = rows - 1
    row(end, True)
    cell = load_cell(cell_ref, end)
    bottom = load_columns(spike_ref, 25 * end, 5) + load_columns(factor_ref, 25 * end, 5)
    side = [to_conserved(advect(col, cell[0] + eps, cell[5]), cell) for col in bottom]
    emit_list(keep_ref, send_ref, bits_ref[0], flatten(side))


def chain_kernel(rows, half, bits_ref, factor_ref, spike_ref, cell_ref, chain_ref, keep_ref, send_ref):
    eps = DAMPING / half
    store_columns(chain_ref, 0, load_columns(factor_ref, 0, 5))

    def inner(i, sums):
        chain = load_columns(chain_ref, 25 * (i - 1), 5)
        out = []
        for c in range(5):
            new = load_columns(spike_ref, 25 * i + 5 * c, 1)[0]
            out += vadd(sums[5 * c : 5 * c + 5], matvec(chain, new))
        for c in range(5):
            new = load_columns(factor_ref, 25 * i + 5 * c, 1)[0]
            store_columns(chain_ref, 25 * i + 5 * c, [matvec(chain, new)])
        return out

    sums = lax.fori_loop(1, rows, inner, flatten(load_columns(spike_ref, 0, 5)))
    cell = load_cell(cell_ref, 0)
    top = [sums[5 * c : 5 * c + 5] for c in range(5)]
    top += load_columns(chain_ref, 25 * (rows - 1), 5)
    side = [[-e for e in to_conserved(advect(col, cell[0] - eps, cell[5]), cell)] for col in top]
    emit_list(keep_ref, send_ref, bits_ref[0], flatten(side))


def right_kernel(
    rows, half, bits_ref, state_ref, cell_ref, lu_ref, chain_ref, left_ref, right_ref,
    part_ref, keep_ref, send_ref, halo_ref,
):
    planes = state_ref.shape[1] // rows
    lanes = state_ref.shape[2]
    diag, eps, scale = DIAGONAL / half, DAMPING / half, 1.0 / half
    lane = lax.broadcasted_iota(jnp.int32, (planes, lanes), 1)
    plane = lax.broadcasted_iota(jnp.int32, (planes, lanes), 0)
    selector = edge_selector(lanes)
    filler = jnp.zeros((8 - 2 * EDGE, planes * rows), jnp.float32)
    for c in range(5):
        edges = jnp.concatenate([right_ref[c], left_ref[c], filler], axis=0)
        halo_ref[c] = lax.dot_general(
            edges, selector, (((0,), (0,)), ((), ())),
            precision=lax.Precision.HIGHEST, preferred_element_type=jnp.float32,
        )

    def prepare(i, carry):
        fields = load_state(state_ref, i, planes, rows)
        cell = load_cell(cell_ref, i)
        own = flux_along(fields, cell, 2)
        outer_fields = load_state(halo_ref, i, planes, rows)
        outer = flux_along(outer_fields, primitives(outer_fields), 2)
        normal = flux_along(fields, cell, 3)
        q = []
        for c in range(5):
            plus1 = pltpu.roll(jnp.where(lane < 1, outer[c], own[c]), lanes - 1, 1)
            plus2 = pltpu.roll(jnp.where(lane < 2, outer[c], own[c]), lanes - 2, 1)
            less1 = pltpu.roll(jnp.where(lane >= lanes - 1, outer[c], own[c]), 1, 1)
            less2 = pltpu.roll(jnp.where(lane >= lanes - 2, outer[c], own[c]), 2, 1)
            span = (less2 - plus2 + 8.0 * (plus1 - less1)) / 12.0
            mirror = normal[c] if c == 3 else -normal[c]
            below = jnp.where(plane == 0, mirror, pltpu.roll(normal[c], 1, 0))
            above = jnp.where(plane == planes - 1, normal[c], pltpu.roll(normal[c], planes - 1, 0))
            q.append(-span - 0.5 * (above - below))
        right = to_primitive(q, cell)
        right[0] = right[0] + fields[0]
        right[4] = right[4] + cell[4]
        for c in range(5):
            part_ref[5 * i + c] = right[c] * scale
        return carry

    lax.fori_loop(0, rows, prepare, 0)
    part = [e * (1.0 / diag) for e in load_columns(part_ref, 0, 1)[0]]
    store_columns(part_ref, 0, [part])

    def inner(i, carry):
        part, const = carry[:5], carry[5:]
        before, here = load_cell(cell_ref, i - 1), load_cell(cell_ref, i)
        moved = shift_frame(
            advect(part, before[0] + eps, before[5]), differences(here, before)
        )
        lu = load_columns(lu_ref, 25 * i, 5)
        factors = lu, [lu[r][r] for r in range(5)]
        part = resolve(factors, vadd(load_columns(part_ref, 5 * i, 1)[0], moved))
        store_columns(part_ref, 5 * i, [part])
        const = vadd(const, matvec(load_columns(chain_ref, 25 * (i - 1), 5), part))
        return part + const

    end = rows - 1
    carry = lax.fori_loop(1, rows, inner, part + part)
    part, const = carry[:5], carry[5:]
    first_cell, last_cell = load_cell(cell_ref, 0), load_cell(cell_ref, end)
    const1 = to_conserved(advect(part, last_cell[0] + eps, last_cell[5]), last_cell)
    const0 = to_conserved(advect(const, first_cell[0] - eps, first_cell[5]), first_cell)
    values = [-e for e in const0] + const1
    values += load_state(state_ref, 0, planes, rows) + load_state(state_ref, end, planes, rows)
    emit_list(keep_ref, send_ref, bits_ref[0], values)


def finish_kernel(
    rows, half, bits_ref, state_ref, factor_ref, spike_ref, part_ref, kept_ref, came_ref,
    next_ref, flux_ref,
):
    planes = state_ref.shape[1] // rows
    eps = DAMPING / half
    bit = bits_ref[0]
    mine = [join_halves(kept_ref[e], came_ref[e], bit, planes) for e in range(20)]
    low_in, high_in, low_n, high_n = (mine[5 * g : 5 * g + 5] for g in range(4))

    load = load_columns

    def step(k, carry):
        i = rows - 1 - k
        w, flux1, flux2 = carry
        spike, factor = load(spike_ref, 25 * i, 5), load(factor_ref, 25 * i, 5)
        part = load(part_ref, 5 * i, 1)[0]
        w = vadd(vadd(part, matvec(spike, low_in)), matvec(factor, w))
        fields = [state_ref[c, pl.ds(i, planes, stride=rows), :] for c in range(5)]
        u, v, speed_w, kinetic, pressure, inverse = primitives(fields)
        cell = (u, v, speed_w, kinetic)
        value = to_conserved(w, cell)
        flux0 = to_conserved(advect(w, u, GAMMA * pressure * inverse), cell)
        for c in range(5):
            next_ref[c, pl.ds(i, planes, stride=rows), :] = value[c]

        @pl.when(k > 0)
        def _():
            for c in range(5):
                flux_ref[c, pl.ds(i + 1, planes, stride=rows), :] = 0.5 * (flux0[c] - flux2[c])

        return w, flux0, flux1

    outer = [eps * n - g for n, g in zip(high_n, high_in)]
    zero = [jnp.zeros_like(e) for e in outer]
    _, flux1, flux2 = lax.fori_loop(0, rows, step, (high_in, outer, zero))
    inner = [g - eps * n for n, g in zip(low_n, low_in)]
    for c in range(5):
        flux_ref[c, pl.ds(0, planes, stride=rows), :] = 0.5 * (inner[c] - flux2[c])


def call(kernel, out_shapes, scratch=()):
    vmem = pl.BlockSpec(memory_space=pltpu.VMEM)

    def run(bits, *args):
        return pl.pallas_call(
            kernel,
            out_shape=[jax.ShapeDtypeStruct(s, jnp.float32) for s in out_shapes],
            in_specs=[pl.BlockSpec(memory_space=pltpu.SMEM)] + [vmem] * len(args),
            out_specs=[vmem] * len(out_shapes),
            compiler_params=pltpu.CompilerParams(vmem_limit_bytes=16 << 20),
            scratch_shapes=[pltpu.VMEM(s, jnp.float32) for s in scratch],
        )(bits, *args)

    return run


def on_device(state):
    fields, planes, rows, lanes = state.shape
    half = 0.5 * 4.0 * rows
    eps = DAMPING / half
    size = lax.axis_size("stream")
    levels = size.bit_length() - 1
    place = lax.axis_index("stream")
    bits = jnp.stack([(place >> l) & 1 for l in range(levels)]).astype(jnp.int32)

    def swap(array, level):
        return lax.ppermute(array, "stream", [(s, s ^ (1 << level)) for s in range(size)])

    flat = (fields, planes * rows, lanes)
    tile = (planes, lanes)
    shapes = [tile]
    for _ in range(levels - 1):
        shapes.append(half_shape(shapes[-1]))
    state_rows = state.reshape(flat)
    store = (25 * rows, *tile)
    edge = (fields, EDGE, planes * rows)
    part_of = lambda n: [(n, *shapes[1])] * 2
    factor, spike, lu, cells, head, tail, own1, sent1 = call(
        functools.partial(sweep_kernel, rows, half),
        [store, store, store, (CELL * rows, *tile), edge, edge] + part_of(MATRIX),
    )(bits, state_rows)
    came1 = swap(sent1, 0)
    span = lax.axis_size("span")
    up = [(i, (i + 1) % span) for i in range(span)]
    left = lax.ppermute(tail, "span", up)
    right = lax.ppermute(head, "span", [(j, i) for i, j in up])
    chain, own0, sent0 = call(
        functools.partial(chain_kernel, rows, half), [store] + part_of(MATRIX)
    )(bits, factor, spike, cells)
    came0 = swap(sent0, 0)
    part, own2, sent2 = call(
        functools.partial(right_kernel, rows, half),
        [(5 * rows, *tile)] + part_of(VECTOR),
        [flat],
    )(bits, state_rows, cells, lu, chain, left, right)
    came2 = swap(sent2, 0)
    own, came = [own0, own1, own2], [came0, came1, came2]
    sizes = [MATRIX, MATRIX, VECTOR]
    faces = []
    for level in range(levels - 1):
        top = level == levels - 2
        out = (35, *shapes[level + 1]) if top else (PORT, *shapes[level + 2])
        kept, sent, face = call(
            functools.partial(merge_kernel, level, top, sizes),
            [out, out, (PORT, *shapes[level + 1])],
        )(bits, *own, *came)
        faces.append(face)
        if not top:
            own, came, sizes = [kept], [swap(sent, level + 1)], [PORT]
    own = kept
    came = swap(sent, levels - 1)
    out = [(20, *shapes[levels - 1])] * 2
    own, sent = call(functools.partial(top_kernel, levels - 1, eps), out)(
        bits, own, came, faces[levels - 2]
    )
    for level in reversed(range(levels - 2)):
        came = swap(sent, level + 1)
        own, sent = call(
            functools.partial(down_kernel, level, eps, shapes[level + 1][0]),
            [(20, *shapes[level + 1])] * 2,
        )(bits, own, came, faces[level])
    came = swap(sent, 0)
    state_next, flux_difference = call(
        functools.partial(finish_kernel, rows, half), [flat, flat]
    )(bits, state_rows, factor, spike, part, own, came)
    return state_next.reshape(state.shape), flux_difference.reshape(state.shape)


def solution(mesh):
    spec = P(None, None, "stream", "span")
    return jax.shard_map(
        on_device, mesh=mesh, in_specs=(spec,), out_specs=(spec, spec), check_vma=False
    )
```

```python
import functools

import jax
import jax.numpy as jnp
from jax import lax
from jax.experimental import pallas as pl
from jax.experimental.pallas import tpu as pltpu
from jax.sharding import PartitionSpec as P

GAMMA = 1.4
GAMMA_LESS = 0.4
DAMPING = 0.125
DIAGONAL = 1.25

MATRIX = 50
VECTOR = 20
PORT = 2 * MATRIX + VECTOR
SIDE = 55
STATES = 110


def add(a, b):
    return b if a is None else a if b is None else a + b


def sub(a, b):
    return a if b is None else -b if a is None else a - b


def mul(a, b):
    return None if a is None or b is None else a * b


def vadd(a, b):
    return [add(x, y) for x, y in zip(a, b)]


def matvec(cols, vec):
    out = []
    for row in range(5):
        acc = None
        for col in range(5):
            acc = add(acc, mul(cols[col][row], vec[col]))
        out.append(acc)
    return out


def factorize(rows):
    rows = [list(row) for row in rows]
    inverse = [None] * 5
    for k in range(5):
        inverse[k] = 1.0 / rows[k][k]
        for i in range(k + 1, 5):
            rows[i][k] = rows[i][k] * inverse[k]
            for j in range(k + 1, 5):
                rows[i][j] = sub(rows[i][j], mul(rows[i][k], rows[k][j]))
    return rows, inverse


def resolve(factors, vec):
    rows, inverse = factors
    x = list(vec)
    for i in range(5):
        for k in range(i):
            x[i] = sub(x[i], mul(rows[i][k], x[k]))
    for i in reversed(range(5)):
        for k in range(i + 1, 5):
            x[i] = sub(x[i], mul(rows[i][k], x[k]))
        x[i] = mul(x[i], inverse[i])
    return x


def primitives(fields):
    density, mom_x, mom_y, mom_z, energy = fields
    inverse = 1.0 / density
    u, v, w = mom_x * inverse, mom_y * inverse, mom_z * inverse
    kinetic = 0.5 * (u * u + v * v + w * w)
    pressure = GAMMA_LESS * (energy - density * kinetic)
    return u, v, w, kinetic, pressure, inverse


def differences(here, there):
    du, dv, dw = (b - a for a, b in zip(here[:3], there[:3]))
    half_square = 0.5 * GAMMA_LESS * (du * du + dv * dv + dw * dw)
    return du, dv, dw, half_square, GAMMA_LESS * du, GAMMA_LESS * dv, GAMMA_LESS * dw


def shift_frame(t, diff):
    du, dv, dw, half_square, du4, dv4, dw4 = diff
    return [
        t[0],
        t[1] + du * t[0],
        t[2] + dv * t[0],
        t[3] + dw * t[0],
        t[4] + half_square * t[0] + (du4 * t[1] + dv4 * t[2] + dw4 * t[3]),
    ]


def advect(x, speed, sound):
    return [
        speed * x[0] + x[1],
        speed * x[1] + x[4],
        speed * x[2],
        speed * x[3],
        speed * x[4] + sound * x[1],
    ]


def to_conserved(z, cell):
    u, v, w, kinetic = cell[:4]
    return [
        z[0],
        u * z[0] + z[1],
        v * z[0] + z[2],
        w * z[0] + z[3],
        kinetic * z[0] + u * z[1] + v * z[2] + w * z[3] + (1.0 / GAMMA_LESS) * z[4],
    ]


def to_primitive(x, cell):
    u, v, w, kinetic = cell[:4]
    return [
        x[0],
        x[1] - u * x[0],
        x[2] - v * x[0],
        x[3] - w * x[0],
        GAMMA_LESS * (kinetic * x[0] - u * x[1] - v * x[2] - w * x[3] + x[4]),
    ]


def primitive_columns(cell):
    u, v, w, kinetic = cell[:4]
    one = jnp.ones_like(u)
    return [
        [one, -u, -v, -w, GAMMA_LESS * kinetic],
        [None, one, None, None, -GAMMA_LESS * u],
        [None, None, one, None, -GAMMA_LESS * v],
        [None, None, None, one, -GAMMA_LESS * w],
        [None, None, None, None, GAMMA_LESS * one],
    ]


def upper_columns(diff, speed, sound):
    du, dv, dw, half_square, du4, dv4, dw4 = diff
    less = -speed
    one = jnp.ones_like(speed)
    return [
        [less, du * less, dv * less, dw * less, half_square * less],
        [-one, -(du + speed), -dv, -dw, du4 * less - (half_square + sound)],
        [None, None, less, None, dv4 * less],
        [None, None, None, less, dw4 * less],
        [None, -one, None, None, -(du4 + speed)],
    ]


def neighbour_value(coupling, fields, eps):
    u, v, w, kinetic, pressure, inverse = primitives(fields)
    z = to_primitive(coupling, (u, v, w, kinetic))
    speed = u + eps
    sound = GAMMA * pressure * inverse
    over = 1.0 / speed
    det = 1.0 / (speed * speed - sound)
    w1 = (speed * z[1] - z[4]) * det
    w4 = (speed * z[4] - sound * z[1]) * det
    return to_conserved([(z[0] - w1) * over, w1, z[2] * over, z[3] * over, w4], (u, v, w, kinetic))


def flux_along(fields, cell, direction):
    pressure = cell[4]
    normal = cell[direction - 1]
    columns = [normal * fields[m] for m in range(4)]
    columns.append(normal * (fields[4] + pressure))
    columns[direction] = columns[direction] + pressure
    return columns


def place_bit(level):
    return (lax.axis_index("stream") >> level) & 1


def merge(low, high):
    a1, a2 = low
    b1, b2 = high
    product = [matvec(b1[:5], col) for col in a2[5:10]]
    one = jnp.ones_like(product[0][0])
    system = [[(one if r == c else 0.0) - product[c][r] for c in range(5)] for r in range(5)]
    factors = factorize(system)
    columns = [matvec(b1[:5], col) for col in a2[:5]] + b1[5:10]
    columns.append(vadd(matvec(b1[:5], a2[10]), b1[10]))
    down = [resolve(factors, col) for col in columns]
    up = [matvec(a2[5:10], col) for col in down]
    up = [vadd(up[c], a2[c]) for c in range(5)] + up[5:10] + [vadd(up[10], a2[10])]
    out1 = [matvec(a1[5:10], col) for col in down]
    out1 = [vadd(out1[c], a1[c]) for c in range(5)] + out1[5:10] + [vadd(out1[10], a1[10])]
    out2 = [matvec(b2[:5], col) for col in up]
    out2 = out2[:5] + [vadd(out2[c], b2[c]) for c in range(5, 10)] + [vadd(out2[10], b2[10])]
    return (out1, out2), down, up


def split_halves(value, bit):
    planes, lanes = value.shape
    if planes > 1:
        halves = value[: planes // 2], value[planes // 2 :]
    else:
        halves = value[:, : lanes // 2], value[:, lanes // 2 :]
    return jnp.where(bit == 0, halves[0], halves[1]), jnp.where(bit == 0, halves[1], halves[0])


def join_halves(kept, came, bit, planes):
    axis = 0 if planes > 1 else 1
    low = jnp.where(bit == 0, kept, came)
    high = jnp.where(bit == 0, came, kept)
    return jnp.concatenate([low, high], axis=axis)


def half_shape(shape):
    planes, lanes = shape
    return (planes // 2, lanes) if planes > 1 else (planes, lanes // 2)


def unpack_port(load):
    sides = []
    for s in range(2):
        cols = [[load(MATRIX * s + 5 * c + r) for r in range(5)] for c in range(10)]
        sides.append(cols + [[load(2 * MATRIX + 5 * s + r) for r in range(5)]])
    first = [load(2 * MATRIX + 10 + r) for r in range(5)]
    last = [load(2 * MATRIX + 15 + r) for r in range(5)]
    return sides, first, last


def emit_list(keep_ref, send_ref, bit, values, base=0):
    for e, value in enumerate(values):
        kept, sent = split_halves(value, bit)
        keep_ref[base + e] = kept
        send_ref[base + e] = sent


def flatten(cols):
    return [value for col in cols for value in col]


def emit_split(keep_ref, send_ref, bit, sides, first, last):
    values = flatten(sides[0][:10] + sides[1][:10] + [sides[0][10], sides[1][10], first, last])
    emit_list(keep_ref, send_ref, bit, values)


def piecewise(refs, sizes):
    def load(e):
        for ref, size in zip(refs, sizes):
            if e < size:
                return ref[e]
            e -= size

    return load


def merge_kernel(level, last_level, sizes, *refs):
    count = len(sizes)
    own, came = piecewise(refs[:count], sizes), piecewise(refs[count : 2 * count], sizes)
    keep_ref, send_ref, face_ref = refs[2 * count :]
    bit = place_bit(level)
    low = lambda e: jnp.where(bit == 0, own(e), came(e))
    high = lambda e: jnp.where(bit == 0, came(e), own(e))
    low_sides, first, low_last = unpack_port(low)
    high_sides, high_first, last = unpack_port(high)
    sides, down, up = merge(low_sides, high_sides)
    for c in range(11):
        for r in range(5):
            face_ref[5 * c + r] = down[c][r]
            face_ref[SIDE + 5 * c + r] = up[c][r]
    for r in range(5):
        face_ref[STATES + r] = low_last[r]
        face_ref[STATES + 5 + r] = high_first[r]
    if not last_level:
        emit_split(keep_ref, send_ref, place_bit(level + 1), sides, first, last)
        return
    half = place_bit(level + 2)
    pick = lambda a, b: [[jnp.where(half == 0, x, y) for x, y in zip(p, q)] for p, q in zip(a, b)]
    mirror = lambda cols: cols[5:10] + cols[:5] + cols[10:]
    near, far = pick(sides[0], mirror(sides[1])), pick(sides[1], mirror(sides[0]))
    ends = pick([first, last], [last, first])
    for e, value in enumerate(flatten(near + far + ends)):
        keep_ref[e] = value
    for e, value in enumerate(flatten(far[5:] + ends[1:])):
        send_ref[e] = value


def inner_kernel(own_ref, came_ref, face_ref, open_ref, send_ref):
    own = [[own_ref[5 * c + r] for r in range(5)] for c in range(24)]
    near, far, far_end = own[:11], own[11:22], own[23]
    outer = [[came_ref[5 * c + r] for r in range(5)] for c in range(7)]
    mirror, shift, outer_end = outer[:5], outer[5], outer[6]
    product = [matvec(near[:5], col) for col in mirror]
    system = [[(1.0 if r == c else 0.0) - product[c][r] for c in range(5)] for r in range(5)]
    factors = factorize(system)
    right = near[5:10] + [vadd(matvec(near[:5], shift), near[10])]
    out = [resolve(factors, col) for col in right]
    back = [matvec(mirror, col) for col in out]
    back[5] = vadd(back[5], shift)
    for e, value in enumerate(flatten(out + back + [outer_end, own[22]])):
        face_ref[e] = value
    wide = [vadd(matvec(far[:5], b), f) for b, f in zip(back, far[5:11])]
    for e, value in enumerate(flatten(wide + [far_end])):
        open_ref[e] = value
        send_ref[e] = value


def middle_kernel(level, eps, open_ref, came_ref, face_ref, own_out, sent_out):
    load = lambda ref, n: [[ref[5 * c + r] for r in range(5)] for c in range(n)]
    here, there, face = load(open_ref, 6), load(came_ref, 7), load(face_ref, 14)
    product = [matvec(here[:5], col) for col in there[:5]]
    system = [[(1.0 if r == c else 0.0) - product[c][r] for c in range(5)] for r in range(5)]
    right = vadd(matvec(here[:5], there[5]), here[5])
    enter = vadd(matvec(there[:5], resolve(factorize(system), right)), there[5])
    out = vadd(matvec(face[:5], enter), face[5])
    back = vadd(matvec(face[6:11], enter), face[11])
    sign = jnp.where(place_bit(level) == 0, 1.0, -1.0)
    signed = lambda col, s: [s * e for e in col]
    n_near = neighbour_value(signed(back, sign), face[12], sign * eps)
    n_far = neighbour_value(signed(enter, -sign), there[6], -sign * eps)
    n_out = neighbour_value(signed(out, -sign), face[13], -sign * eps)
    for e, value in enumerate(flatten([back, enter, n_near, n_far])):
        own_out[e] = value
    for e, value in enumerate(flatten([out, n_out])):
        sent_out[e] = value


def descend(bit, face_ref, values, eps, own_ref, partner_ref):
    low_in, high_in, low_n, high_n = values
    down, up = (
        [[face_ref[s * SIDE + 5 * c + r] for r in range(5)] for c in range(11)] for s in range(2)
    )
    from_high = vadd(vadd(matvec(down[:5], low_in), matvec(down[5:10], high_in)), down[10])
    from_low = vadd(vadd(matvec(up[:5], low_in), matvec(up[5:10], high_in)), up[10])
    low_last = [face_ref[STATES + r] for r in range(5)]
    high_first = [face_ref[STATES + 5 + r] for r in range(5)]
    n_low = neighbour_value(from_low, low_last, eps)
    n_high = neighbour_value([-e for e in from_high], high_first, -eps)
    as_low = low_in + from_high + low_n + n_high
    as_high = from_low + high_in + n_low + high_n
    for e in range(20):
        own_ref[e] = jnp.where(bit == 0, as_low[e], as_high[e])
        partner_ref[e] = jnp.where(bit == 0, as_high[e], as_low[e])


def blocks_kernel(level, eps, inner_ref, came_ref, face_ref, own_out, partner_out):
    half = place_bit(level + 2)
    inner = place_bit(level + 1) != half
    zero = jnp.zeros(came_ref.shape[1:], came_ref.dtype)
    near, far, n_near, n_far = (
        [jnp.where(inner, inner_ref[5 * g + r], outer(r)) for r in range(5)]
        for g, outer in enumerate(
            (
                lambda r: zero,
                lambda r: came_ref[r],
                lambda r: zero,
                lambda r: came_ref[5 + r],
            )
        )
    )
    pick = lambda a, b: [jnp.where(half == 0, x, y) for x, y in zip(a, b)]
    values = [pick(near, far), pick(far, near), pick(n_near, n_far), pick(n_far, n_near)]
    descend(place_bit(level), face_ref, values, eps, own_out, partner_out)


def down_kernel(level, eps, planes, kept_ref, came_ref, face_ref, own_out, partner_out):
    bit = place_bit(level + 1)
    mine = [join_halves(kept_ref[e], came_ref[e], bit, planes) for e in range(20)]
    values = [mine[5 * g : 5 * g + 5] for g in range(4)]
    descend(place_bit(level), face_ref, values, eps, own_out, partner_out)


CELL = 6
EDGE = 2


def load_columns(ref, base, count):
    return [[ref[base + 5 * c + r] for r in range(5)] for c in range(count)]


def store_columns(ref, base, cols):
    for c in range(len(cols)):
        for r in range(5):
            value = cols[c][r]
            ref[base + 5 * c + r] = jnp.zeros(ref.shape[1:], ref.dtype) if value is None else value


def load_cell(ref, i):
    return [ref[CELL * i + c] for c in range(CELL)]


def load_state(ref, i, planes, rows):
    return [ref[c, pl.ds(i, planes, stride=rows), :] for c in range(5)]


def sweep_kernel(
    rows, half, state_ref, factor_ref, spike_ref, lu_ref, cell_ref, head_ref, tail_ref,
    keep_ref, send_ref,
):
    planes = state_ref.shape[1] // rows
    lanes = state_ref.shape[2]
    diag, eps = DIAGONAL / half, DAMPING / half
    lane = lax.broadcasted_iota(jnp.int32, (planes, lanes), 1)

    def prepare(i):
        fields = load_state(state_ref, i, planes, rows)
        spot = EDGE * i
        mine = (lane >= spot) & (lane < spot + EDGE)
        for c in range(5):
            head = pltpu.roll(fields[c], spot, 1)
            tail = pltpu.roll(fields[c], spot + EDGE, 1)
            head_ref[c] = jnp.where(mine, head, head_ref[c])
            tail_ref[c] = jnp.where(mine, tail, tail_ref[c])
        u, v, w, kinetic, pressure, inverse = primitives(fields)
        cell = (u, v, w, kinetic, pressure, GAMMA * pressure * inverse)
        for c, value in enumerate(cell):
            cell_ref[CELL * i + c] = value
        return cell

    for c in range(5):
        head_ref[c] = tail_ref[c] = state_ref[c, pl.ds(0, planes, stride=rows), :]
    here, after = prepare(0), prepare(1)
    inv = 1.0 / diag
    upper = upper_columns(differences(here, after), after[0] - eps, after[5])
    store_columns(factor_ref, 0, [[mul(e, inv) for e in col] for col in upper])
    store_columns(spike_ref, 0, [[mul(e, inv) for e in col] for col in primitive_columns(here)])

    def row(i, final):
        before, here = load_cell(cell_ref, i - 1), load_cell(cell_ref, i)
        diff = differences(here, before)
        speed, sound = before[0] + eps, before[5]
        lower = lambda col: shift_frame(advect(col, speed, sound), diff)
        moved = [lower(col) for col in load_columns(factor_ref, 25 * (i - 1), 5)]
        pivot = [[(diag - moved[c][r]) if r == c else -moved[c][r] for c in range(5)] for r in range(5)]
        factors = factorize(pivot)
        for r in range(5):
            for c in range(5):
                lu_ref[25 * i + 5 * r + c] = factors[1][r] if r == c else factors[0][r][c]
        if final:
            upper = primitive_columns(here)
        else:
            after = prepare(i + 1)
            upper = upper_columns(differences(here, after), after[0] - eps, after[5])
        store_columns(factor_ref, 25 * i, [resolve(factors, col) for col in upper])
        spike = [resolve(factors, lower(col)) for col in load_columns(spike_ref, 25 * (i - 1), 5)]
        store_columns(spike_ref, 25 * i, spike)

    def inner(i, carry):
        row(i, False)
        return carry

    lax.fori_loop(1, rows - 1, inner, 0)
    end = rows - 1
    row(end, True)
    cell = load_cell(cell_ref, end)
    bottom = load_columns(spike_ref, 25 * end, 5) + load_columns(factor_ref, 25 * end, 5)
    side = [to_conserved(advect(col, cell[0] + eps, cell[5]), cell) for col in bottom]
    emit_list(keep_ref, send_ref, place_bit(0), flatten(side))


def chain_kernel(rows, half, factor_ref, spike_ref, cell_ref, chain_ref, keep_ref, send_ref):
    eps = DAMPING / half
    store_columns(chain_ref, 0, load_columns(factor_ref, 0, 5))

    def inner(i, sums):
        chain = load_columns(chain_ref, 25 * (i - 1), 5)
        out = []
        for c in range(5):
            new = load_columns(spike_ref, 25 * i + 5 * c, 1)[0]
            out += vadd(sums[5 * c : 5 * c + 5], matvec(chain, new))
        for c in range(5):
            new = load_columns(factor_ref, 25 * i + 5 * c, 1)[0]
            store_columns(chain_ref, 25 * i + 5 * c, [matvec(chain, new)])
        return out

    sums = lax.fori_loop(1, rows, inner, flatten(load_columns(spike_ref, 0, 5)))
    cell = load_cell(cell_ref, 0)
    top = [sums[5 * c : 5 * c + 5] for c in range(5)]
    top += load_columns(chain_ref, 25 * (rows - 1), 5)
    side = [[-e for e in to_conserved(advect(col, cell[0] - eps, cell[5]), cell)] for col in top]
    emit_list(keep_ref, send_ref, place_bit(0), flatten(side))


def right_kernel(
    rows, half, state_ref, cell_ref, lu_ref, chain_ref, left_ref, right_ref,
    part_ref, keep_ref, send_ref, halo_ref,
):
    planes = state_ref.shape[1] // rows
    lanes = state_ref.shape[2]
    diag, eps, scale = DIAGONAL / half, DAMPING / half, 1.0 / half
    lane = lax.broadcasted_iota(jnp.int32, (planes, lanes), 1)
    plane = lax.broadcasted_iota(jnp.int32, (planes, lanes), 0)
    for side, ref in enumerate((right_ref, left_ref)):
        fields = [ref[c] for c in range(5)]
        for c, value in enumerate(flux_along(fields, primitives(fields), 2)):
            halo_ref[5 * side + c] = value

    def prepare(i, carry):
        fields = load_state(state_ref, i, planes, rows)
        cell = load_cell(cell_ref, i)
        own = flux_along(fields, cell, 2)
        after = lax.rem(lanes - EDGE * i, lanes)
        before = lanes - EDGE * (i + 1)
        normal = flux_along(fields, cell, 3)
        q = []
        for c in range(5):
            above = pltpu.roll(halo_ref[c], after, 1)
            below = pltpu.roll(halo_ref[5 + c], before, 1)
            plus1 = pltpu.roll(jnp.where(lane < 1, above, own[c]), lanes - 1, 1)
            plus2 = pltpu.roll(jnp.where(lane < 2, above, own[c]), lanes - 2, 1)
            less1 = pltpu.roll(jnp.where(lane >= lanes - 1, below, own[c]), 1, 1)
            less2 = pltpu.roll(jnp.where(lane >= lanes - 2, below, own[c]), 2, 1)
            span = (less2 - plus2 + 8.0 * (plus1 - less1)) / 12.0
            mirror = normal[c] if c == 3 else -normal[c]
            below = jnp.where(plane == 0, mirror, pltpu.roll(normal[c], 1, 0))
            above = jnp.where(plane == planes - 1, normal[c], pltpu.roll(normal[c], planes - 1, 0))
            q.append(-span - 0.5 * (above - below))
        right = to_primitive(q, cell)
        right[0] = right[0] + fields[0]
        right[4] = right[4] + cell[4]
        for c in range(5):
            part_ref[5 * i + c] = right[c] * scale
        return carry

    lax.fori_loop(0, rows, prepare, 0)
    part = [e * (1.0 / diag) for e in load_columns(part_ref, 0, 1)[0]]
    store_columns(part_ref, 0, [part])

    def inner(i, carry):
        part, const = carry[:5], carry[5:]
        before, here = load_cell(cell_ref, i - 1), load_cell(cell_ref, i)
        moved = shift_frame(
            advect(part, before[0] + eps, before[5]), differences(here, before)
        )
        lu = load_columns(lu_ref, 25 * i, 5)
        factors = lu, [lu[r][r] for r in range(5)]
        part = resolve(factors, vadd(load_columns(part_ref, 5 * i, 1)[0], moved))
        store_columns(part_ref, 5 * i, [part])
        const = vadd(const, matvec(load_columns(chain_ref, 25 * (i - 1), 5), part))
        return part + const

    end = rows - 1
    carry = lax.fori_loop(1, rows, inner, part + part)
    part, const = carry[:5], carry[5:]
    first_cell, last_cell = load_cell(cell_ref, 0), load_cell(cell_ref, end)
    const1 = to_conserved(advect(part, last_cell[0] + eps, last_cell[5]), last_cell)
    const0 = to_conserved(advect(const, first_cell[0] - eps, first_cell[5]), first_cell)
    values = [-e for e in const0] + const1
    values += load_state(state_ref, 0, planes, rows) + load_state(state_ref, end, planes, rows)
    emit_list(keep_ref, send_ref, place_bit(0), values)


def finish_kernel(
    rows, half, state_ref, factor_ref, spike_ref, part_ref, kept_ref, came_ref,
    next_ref, flux_ref,
):
    planes = state_ref.shape[1] // rows
    eps = DAMPING / half
    bit = place_bit(0)
    mine = [join_halves(kept_ref[e], came_ref[e], bit, planes) for e in range(20)]
    low_in, high_in, low_n, high_n = (mine[5 * g : 5 * g + 5] for g in range(4))

    load = load_columns

    def step(k, carry):
        i = rows - 1 - k
        w, flux1, flux2 = carry
        spike, factor = load(spike_ref, 25 * i, 5), load(factor_ref, 25 * i, 5)
        part = load(part_ref, 5 * i, 1)[0]
        w = vadd(vadd(part, matvec(spike, low_in)), matvec(factor, w))
        fields = [state_ref[c, pl.ds(i, planes, stride=rows), :] for c in range(5)]
        u, v, speed_w, kinetic, pressure, inverse = primitives(fields)
        cell = (u, v, speed_w, kinetic)
        value = to_conserved(w, cell)
        flux0 = to_conserved(advect(w, u, GAMMA * pressure * inverse), cell)
        for c in range(5):
            next_ref[c, pl.ds(i, planes, stride=rows), :] = value[c]

        @pl.when(k > 0)
        def _():
            for c in range(5):
                flux_ref[c, pl.ds(i + 1, planes, stride=rows), :] = 0.5 * (flux0[c] - flux2[c])

        return w, flux0, flux1

    outer = [eps * n - g for n, g in zip(high_n, high_in)]
    zero = [jnp.zeros_like(e) for e in outer]
    _, flux1, flux2 = lax.fori_loop(0, rows, step, (high_in, outer, zero))
    inner = [g - eps * n for n, g in zip(low_n, low_in)]
    for c in range(5):
        flux_ref[c, pl.ds(0, planes, stride=rows), :] = 0.5 * (inner[c] - flux2[c])


def call(kernel, out_shapes, scratch=()):
    vmem = pl.BlockSpec(memory_space=pltpu.VMEM)

    def run(*args):
        return pl.pallas_call(
            kernel,
            out_shape=[jax.ShapeDtypeStruct(s, jnp.float32) for s in out_shapes],
            in_specs=[vmem] * len(args),
            out_specs=[vmem] * len(out_shapes),
            compiler_params=pltpu.CompilerParams(vmem_limit_bytes=16 << 20),
            scratch_shapes=[pltpu.VMEM(s, jnp.float32) for s in scratch],
        )(*args)

    return run


def on_device(state):
    fields, planes, rows, lanes = state.shape
    half = 0.5 * 4.0 * rows
    eps = DAMPING / half
    size = lax.axis_size("stream")
    levels = size.bit_length() - 1
    flat = (fields, planes * rows, lanes)
    tile = (planes, lanes)
    store = (25 * rows, *tile)
    edge = (fields, *tile)
    shapes = [tile]
    for _ in range(levels - 2):
        shapes.append(half_shape(shapes[-1]))
    lines = shapes[-1]
    halves = lambda n: [(n, *shapes[1])] * 2

    def swap(array, level):
        return lax.ppermute(array, "stream", [(s, s ^ (1 << level)) for s in range(size)])

    def move(array, pairs):
        block = size // 4
        pairs = [(a * block + s, b * block + s) for a, b in pairs for s in range(block)]
        return lax.ppermute(array, "stream", pairs)

    state_rows = state.reshape(flat)
    factor, spike, lu, cells, head, tail, own1, sent1 = call(
        functools.partial(sweep_kernel, rows, half),
        [store, store, store, (CELL * rows, *tile), edge, edge] + halves(MATRIX),
    )(state_rows)
    span = lax.axis_size("span")
    up = [(i, (i + 1) % span) for i in range(span)]
    with jax.named_scope("halo_up"):
        left = lax.ppermute(tail, "span", up)
    with jax.named_scope("halo_down"):
        right = lax.ppermute(head, "span", [(j, i) for i, j in up])
    with jax.named_scope("swap_side1"):
        came1 = swap(sent1, 0)
    with jax.named_scope("chain"):
        chain, own0, sent0 = call(
            functools.partial(chain_kernel, rows, half), [store] + halves(MATRIX)
        )(factor, spike, cells)
    with jax.named_scope("swap_side0"):
        came0 = swap(sent0, 0)
    with jax.named_scope("right"):
        part, own2, sent2 = call(
            functools.partial(right_kernel, rows, half),
            [(5 * rows, *tile)] + halves(VECTOR),
            [(10, *tile)],
        )(state_rows, cells, lu, chain, left, right)
    came2 = swap(sent2, 0)
    own, came = [own0, own1, own2], [came0, came1, came2]
    sizes = [MATRIX, MATRIX, VECTOR]
    faces = []
    for level in range(levels - 2):
        last = level == levels - 3
        outs = [(PORT, *lines), (35, *lines)] if last else [(PORT, *shapes[level + 2])] * 2
        kept, sent, face = call(
            functools.partial(merge_kernel, level, last, sizes),
            outs + [(PORT, *shapes[level + 1])],
        )(*own, *came)
        faces.append(face)
        if not last:
            own, came, sizes = [kept], [swap(sent, level + 1)], [PORT]
    came = move(sent, [(0, 1), (3, 2)])
    face, opened, sent = call(inner_kernel, [(70, *lines), (35, *lines), (35, *lines)])(kept, came)
    came = move(sent, [(1, 2), (2, 1)])
    inner, sent = call(
        functools.partial(middle_kernel, levels - 1, eps), [(20, *lines), (10, *lines)]
    )(opened, came, face)
    came = move(sent, [(1, 0), (2, 3)])
    own, sent = call(
        functools.partial(blocks_kernel, levels - 3, eps), [(20, *lines)] * 2
    )(inner, came, faces[-1])
    for level in reversed(range(levels - 3)):
        came = swap(sent, level + 1)
        own, sent = call(
            functools.partial(down_kernel, level, eps, shapes[level + 1][0]),
            [(20, *shapes[level + 1])] * 2,
        )(own, came, faces[level])
    came = swap(sent, 0)
    state_next, flux_difference = call(
        functools.partial(finish_kernel, rows, half), [flat, flat]
    )(state_rows, factor, spike, part, own, came)
    return state_next.reshape(state.shape), flux_difference.reshape(state.shape)


def solution(mesh):
    spec = P(None, None, "stream", "span")
    return jax.shard_map(
        on_device, mesh=mesh, in_specs=(spec,), out_specs=(spec, spec), check_vma=False
    )
```

```python
import functools

import jax
import jax.numpy as jnp
from jax import lax
from jax.experimental import pallas as pl
from jax.experimental.pallas import tpu as pltpu
from jax.sharding import PartitionSpec as P

GAMMA = 1.4
GAMMA_LESS = 0.4
DAMPING = 0.125
DIAGONAL = 1.25

MATRIX = 50
VECTOR = 20
PORT = 2 * MATRIX + VECTOR
SIDE = 55
STATES = 110


def add(a, b):
    return b if a is None else a if b is None else a + b


def sub(a, b):
    return a if b is None else -b if a is None else a - b


def mul(a, b):
    return None if a is None or b is None else a * b


def vadd(a, b):
    return [add(x, y) for x, y in zip(a, b)]


def matvec(cols, vec):
    out = []
    for row in range(5):
        acc = None
        for col in range(5):
            acc = add(acc, mul(cols[col][row], vec[col]))
        out.append(acc)
    return out


def factorize(rows):
    rows = [list(row) for row in rows]
    inverse = [None] * 5
    for k in range(5):
        inverse[k] = 1.0 / rows[k][k]
        for i in range(k + 1, 5):
            rows[i][k] = rows[i][k] * inverse[k]
            for j in range(k + 1, 5):
                rows[i][j] = sub(rows[i][j], mul(rows[i][k], rows[k][j]))
    return rows, inverse


def resolve(factors, vec):
    rows, inverse = factors
    x = list(vec)
    for i in range(5):
        for k in range(i):
            x[i] = sub(x[i], mul(rows[i][k], x[k]))
    for i in reversed(range(5)):
        for k in range(i + 1, 5):
            x[i] = sub(x[i], mul(rows[i][k], x[k]))
        x[i] = mul(x[i], inverse[i])
    return x


def primitives(fields):
    density, mom_x, mom_y, mom_z, energy = fields
    inverse = 1.0 / density
    u, v, w = mom_x * inverse, mom_y * inverse, mom_z * inverse
    kinetic = 0.5 * (u * u + v * v + w * w)
    pressure = GAMMA_LESS * (energy - density * kinetic)
    return u, v, w, kinetic, pressure, inverse


def differences(here, there):
    du, dv, dw = (b - a for a, b in zip(here[:3], there[:3]))
    half_square = 0.5 * GAMMA_LESS * (du * du + dv * dv + dw * dw)
    return du, dv, dw, half_square, GAMMA_LESS * du, GAMMA_LESS * dv, GAMMA_LESS * dw


def shift_frame(t, diff):
    du, dv, dw, half_square, du4, dv4, dw4 = diff
    return [
        t[0],
        t[1] + du * t[0],
        t[2] + dv * t[0],
        t[3] + dw * t[0],
        t[4] + half_square * t[0] + (du4 * t[1] + dv4 * t[2] + dw4 * t[3]),
    ]


def advect(x, speed, sound):
    return [
        speed * x[0] + x[1],
        speed * x[1] + x[4],
        speed * x[2],
        speed * x[3],
        speed * x[4] + sound * x[1],
    ]


def to_conserved(z, cell):
    u, v, w, kinetic = cell[:4]
    return [
        z[0],
        u * z[0] + z[1],
        v * z[0] + z[2],
        w * z[0] + z[3],
        kinetic * z[0] + u * z[1] + v * z[2] + w * z[3] + (1.0 / GAMMA_LESS) * z[4],
    ]


def to_primitive(x, cell):
    u, v, w, kinetic = cell[:4]
    return [
        x[0],
        x[1] - u * x[0],
        x[2] - v * x[0],
        x[3] - w * x[0],
        GAMMA_LESS * (kinetic * x[0] - u * x[1] - v * x[2] - w * x[3] + x[4]),
    ]


def primitive_columns(cell):
    u, v, w, kinetic = cell[:4]
    one = jnp.ones_like(u)
    return [
        [one, -u, -v, -w, GAMMA_LESS * kinetic],
        [None, one, None, None, -GAMMA_LESS * u],
        [None, None, one, None, -GAMMA_LESS * v],
        [None, None, None, one, -GAMMA_LESS * w],
        [None, None, None, None, GAMMA_LESS * one],
    ]


def upper_columns(diff, speed, sound):
    du, dv, dw, half_square, du4, dv4, dw4 = diff
    less = -speed
    one = jnp.ones_like(speed)
    return [
        [less, du * less, dv * less, dw * less, half_square * less],
        [-one, -(du + speed), -dv, -dw, du4 * less - (half_square + sound)],
        [None, None, less, None, dv4 * less],
        [None, None, None, less, dw4 * less],
        [None, -one, None, None, -(du4 + speed)],
    ]


def neighbour_value(coupling, fields, eps):
    u, v, w, kinetic, pressure, inverse = primitives(fields)
    z = to_primitive(coupling, (u, v, w, kinetic))
    speed = u + eps
    sound = GAMMA * pressure * inverse
    over = 1.0 / speed
    det = 1.0 / (speed * speed - sound)
    w1 = (speed * z[1] - z[4]) * det
    w4 = (speed * z[4] - sound * z[1]) * det
    return to_conserved([(z[0] - w1) * over, w1, z[2] * over, z[3] * over, w4], (u, v, w, kinetic))


def flux_along(fields, cell, direction):
    pressure = cell[4]
    normal = cell[direction - 1]
    columns = [normal * fields[m] for m in range(4)]
    columns.append(normal * (fields[4] + pressure))
    columns[direction] = columns[direction] + pressure
    return columns


def place_bit(level):
    return (lax.axis_index("stream") >> level) & 1


def merge(low, high):
    a1, a2 = low
    b1, b2 = high
    product = [matvec(b1[:5], col) for col in a2[5:10]]
    one = jnp.ones_like(product[0][0])
    system = [[(one if r == c else 0.0) - product[c][r] for c in range(5)] for r in range(5)]
    factors = factorize(system)
    columns = [matvec(b1[:5], col) for col in a2[:5]] + b1[5:10]
    columns.append(vadd(matvec(b1[:5], a2[10]), b1[10]))
    down = [resolve(factors, col) for col in columns]
    up = [matvec(a2[5:10], col) for col in down]
    up = [vadd(up[c], a2[c]) for c in range(5)] + up[5:10] + [vadd(up[10], a2[10])]
    out1 = [matvec(a1[5:10], col) for col in down]
    out1 = [vadd(out1[c], a1[c]) for c in range(5)] + out1[5:10] + [vadd(out1[10], a1[10])]
    out2 = [matvec(b2[:5], col) for col in up]
    out2 = out2[:5] + [vadd(out2[c], b2[c]) for c in range(5, 10)] + [vadd(out2[10], b2[10])]
    return (out1, out2), down, up


def split_halves(value, bit):
    planes, lanes = value.shape
    if planes > 1:
        halves = value[: planes // 2], value[planes // 2 :]
    else:
        halves = value[:, : lanes // 2], value[:, lanes // 2 :]
    return jnp.where(bit == 0, halves[0], halves[1]), jnp.where(bit == 0, halves[1], halves[0])


def join_halves(kept, came, bit, planes):
    axis = 0 if planes > 1 else 1
    low = jnp.where(bit == 0, kept, came)
    high = jnp.where(bit == 0, came, kept)
    return jnp.concatenate([low, high], axis=axis)


def half_shape(shape):
    planes, lanes = shape
    return (planes // 2, lanes) if planes > 1 else (planes, lanes // 2)


def unpack_port(load):
    sides = []
    for s in range(2):
        cols = [[load(MATRIX * s + 5 * c + r) for r in range(5)] for c in range(10)]
        sides.append(cols + [[load(2 * MATRIX + 5 * s + r) for r in range(5)]])
    first = [load(2 * MATRIX + 10 + r) for r in range(5)]
    last = [load(2 * MATRIX + 15 + r) for r in range(5)]
    return sides, first, last


def emit_list(keep_ref, send_ref, bit, values, base=0):
    for e, value in enumerate(values):
        kept, sent = split_halves(value, bit)
        keep_ref[base + e] = kept
        send_ref[base + e] = sent


def flatten(cols):
    return [value for col in cols for value in col]


def emit_split(keep_ref, send_ref, bit, sides, first, last):
    values = flatten(sides[0][:10] + sides[1][:10] + [sides[0][10], sides[1][10], first, last])
    emit_list(keep_ref, send_ref, bit, values)


def piecewise(refs, sizes):
    def load(e):
        for ref, size in zip(refs, sizes):
            if e < size:
                return ref[e]
            e -= size

    return load


def merge_kernel(level, last_level, sizes, *refs):
    count = len(sizes)
    own, came = piecewise(refs[:count], sizes), piecewise(refs[count : 2 * count], sizes)
    keep_ref, send_ref, face_ref = refs[2 * count :]
    bit = place_bit(level)
    low = lambda e: jnp.where(bit == 0, own(e), came(e))
    high = lambda e: jnp.where(bit == 0, came(e), own(e))
    low_sides, first, low_last = unpack_port(low)
    high_sides, high_first, last = unpack_port(high)
    sides, down, up = merge(low_sides, high_sides)
    for c in range(11):
        for r in range(5):
            face_ref[5 * c + r] = down[c][r]
            face_ref[SIDE + 5 * c + r] = up[c][r]
    for r in range(5):
        face_ref[STATES + r] = low_last[r]
        face_ref[STATES + 5 + r] = high_first[r]
    if last_level:
        half = place_bit(level + 2)
        pick = lambda a, b: [[jnp.where(half == 0, x, y) for x, y in zip(p, q)] for p, q in zip(a, b)]
        mirror = lambda cols: cols[5:10] + cols[:5] + cols[10:]
        near, far = pick(sides[0], mirror(sides[1])), pick(sides[1], mirror(sides[0]))
        ends = pick([first, last], [last, first])
        emit_list(keep_ref, send_ref, place_bit(level + 1), flatten(near + far + ends))
    else:
        emit_split(keep_ref, send_ref, place_bit(level + 1), sides, first, last)


def inner_kernel(level, own_ref, came_ref, face_ref, open_ref, send_ref):
    inner = place_bit(level) != place_bit(level + 1)
    load = lambda a, b, c: [jnp.where(inner, a[5 * c + r], b[5 * c + r]) for r in range(5)]
    own = [load(own_ref, came_ref, c) for c in range(24)]
    near, far, far_end = own[:11], own[11:22], own[23]
    outer = [load(came_ref, own_ref, c) for c in (16, 17, 18, 19, 20, 21, 23)]
    mirror, shift, outer_end = outer[:5], outer[5], outer[6]
    product = [matvec(near[:5], col) for col in mirror]
    system = [[(1.0 if r == c else 0.0) - product[c][r] for c in range(5)] for r in range(5)]
    factors = factorize(system)
    right = near[5:10] + [vadd(matvec(near[:5], shift), near[10])]
    out = [resolve(factors, col) for col in right]
    back = [matvec(mirror, col) for col in out]
    back[5] = vadd(back[5], shift)
    for e, value in enumerate(flatten(out + back + [outer_end, own[22]])):
        face_ref[e] = value
    wide = [vadd(matvec(far[:5], b), f) for b, f in zip(back, far[5:11])]
    for e, value in enumerate(flatten(wide + [far_end])):
        open_ref[e] = value
        send_ref[e] = value


def middle_kernel(level, eps, open_ref, came_ref, face_ref, own_out, sent_out):
    load = lambda ref, n: [[ref[5 * c + r] for r in range(5)] for c in range(n)]
    here, there, face = load(open_ref, 6), load(came_ref, 7), load(face_ref, 14)
    product = [matvec(here[:5], col) for col in there[:5]]
    system = [[(1.0 if r == c else 0.0) - product[c][r] for c in range(5)] for r in range(5)]
    right = vadd(matvec(here[:5], there[5]), here[5])
    enter = vadd(matvec(there[:5], resolve(factorize(system), right)), there[5])
    out = vadd(matvec(face[:5], enter), face[5])
    back = vadd(matvec(face[6:11], enter), face[11])
    sign = jnp.where(place_bit(level) == 0, 1.0, -1.0)
    signed = lambda col, s: [s * e for e in col]
    n_near = neighbour_value(signed(back, sign), face[12], sign * eps)
    n_far = neighbour_value(signed(enter, -sign), there[6], -sign * eps)
    n_out = neighbour_value(signed(out, -sign), face[13], -sign * eps)
    half = place_bit(level)
    inner = place_bit(level - 1) != half
    zero = [jnp.zeros_like(e) for e in out]
    pick = lambda a, b: [jnp.where(half == 0, x, y) for x, y in zip(a, b)]
    mid = pick(back, enter) + pick(enter, back) + pick(n_near, n_far) + pick(n_far, n_near)
    rim = pick(zero, out) + pick(out, zero) + pick(zero, n_out) + pick(n_out, zero)
    for e in range(20):
        own_out[e] = jnp.where(inner, mid[e], rim[e])
        sent_out[e] = jnp.where(inner, rim[e], mid[e])


def descend(bit, face_ref, values, eps, own_ref, partner_ref):
    low_in, high_in, low_n, high_n = values
    down, up = (
        [[face_ref[s * SIDE + 5 * c + r] for r in range(5)] for c in range(11)] for s in range(2)
    )
    from_high = vadd(vadd(matvec(down[:5], low_in), matvec(down[5:10], high_in)), down[10])
    from_low = vadd(vadd(matvec(up[:5], low_in), matvec(up[5:10], high_in)), up[10])
    low_last = [face_ref[STATES + r] for r in range(5)]
    high_first = [face_ref[STATES + 5 + r] for r in range(5)]
    n_low = neighbour_value(from_low, low_last, eps)
    n_high = neighbour_value([-e for e in from_high], high_first, -eps)
    as_low = low_in + from_high + low_n + n_high
    as_high = from_low + high_in + n_low + high_n
    for e in range(20):
        own_ref[e] = jnp.where(bit == 0, as_low[e], as_high[e])
        partner_ref[e] = jnp.where(bit == 0, as_high[e], as_low[e])


def down_kernel(level, eps, planes, kept_ref, came_ref, face_ref, own_out, partner_out):
    bit = place_bit(level + 1)
    mine = [join_halves(kept_ref[e], came_ref[e], bit, planes) for e in range(20)]
    values = [mine[5 * g : 5 * g + 5] for g in range(4)]
    descend(place_bit(level), face_ref, values, eps, own_out, partner_out)


CELL = 6
EDGE = 2


def load_columns(ref, base, count):
    return [[ref[base + 5 * c + r] for r in range(5)] for c in range(count)]


def store_columns(ref, base, cols):
    for c in range(len(cols)):
        for r in range(5):
            value = cols[c][r]
            ref[base + 5 * c + r] = jnp.zeros(ref.shape[1:], ref.dtype) if value is None else value


def load_cell(ref, i):
    return [ref[CELL * i + c] for c in range(CELL)]


def load_state(ref, i, planes, rows):
    return [ref[c, pl.ds(i, planes, stride=rows), :] for c in range(5)]


def sweep_kernel(
    rows, half, state_ref, factor_ref, spike_ref, lu_ref, cell_ref, head_ref, tail_ref,
    keep_ref, send_ref,
):
    planes = state_ref.shape[1] // rows
    lanes = state_ref.shape[2]
    diag, eps = DIAGONAL / half, DAMPING / half
    lane = lax.broadcasted_iota(jnp.int32, (planes, lanes), 1)

    def prepare(i):
        fields = load_state(state_ref, i, planes, rows)
        spot = EDGE * i
        mine = (lane >= spot) & (lane < spot + EDGE)
        for c in range(5):
            head = pltpu.roll(fields[c], spot, 1)
            tail = pltpu.roll(fields[c], spot + EDGE, 1)
            head_ref[c] = jnp.where(mine, head, head_ref[c])
            tail_ref[c] = jnp.where(mine, tail, tail_ref[c])
        u, v, w, kinetic, pressure, inverse = primitives(fields)
        cell = (u, v, w, kinetic, pressure, GAMMA * pressure * inverse)
        for c, value in enumerate(cell):
            cell_ref[CELL * i + c] = value
        return cell

    for c in range(5):
        head_ref[c] = tail_ref[c] = state_ref[c, pl.ds(0, planes, stride=rows), :]
    here, after = prepare(0), prepare(1)
    inv = 1.0 / diag
    upper = upper_columns(differences(here, after), after[0] - eps, after[5])
    store_columns(factor_ref, 0, [[mul(e, inv) for e in col] for col in upper])
    store_columns(spike_ref, 0, [[mul(e, inv) for e in col] for col in primitive_columns(here)])

    def row(i, final):
        before, here = load_cell(cell_ref, i - 1), load_cell(cell_ref, i)
        diff = differences(here, before)
        speed, sound = before[0] + eps, before[5]
        lower = lambda col: shift_frame(advect(col, speed, sound), diff)
        moved = [lower(col) for col in load_columns(factor_ref, 25 * (i - 1), 5)]
        pivot = [[(diag - moved[c][r]) if r == c else -moved[c][r] for c in range(5)] for r in range(5)]
        factors = factorize(pivot)
        for r in range(5):
            for c in range(5):
                lu_ref[25 * i + 5 * r + c] = factors[1][r] if r == c else factors[0][r][c]
        if final:
            upper = primitive_columns(here)
        else:
            after = prepare(i + 1)
            upper = upper_columns(differences(here, after), after[0] - eps, after[5])
        store_columns(factor_ref, 25 * i, [resolve(factors, col) for col in upper])
        spike = [resolve(factors, lower(col)) for col in load_columns(spike_ref, 25 * (i - 1), 5)]
        store_columns(spike_ref, 25 * i, spike)

    def inner(i, carry):
        row(i, False)
        return carry

    lax.fori_loop(1, rows - 1, inner, 0)
    end = rows - 1
    row(end, True)
    cell = load_cell(cell_ref, end)
    bottom = load_columns(spike_ref, 25 * end, 5) + load_columns(factor_ref, 25 * end, 5)
    side = [to_conserved(advect(col, cell[0] + eps, cell[5]), cell) for col in bottom]
    emit_list(keep_ref, send_ref, place_bit(0), flatten(side))


def chain_kernel(rows, half, factor_ref, spike_ref, cell_ref, chain_ref, keep_ref, send_ref):
    eps = DAMPING / half
    store_columns(chain_ref, 0, load_columns(factor_ref, 0, 5))

    def inner(i, sums):
        chain = load_columns(chain_ref, 25 * (i - 1), 5)
        out = []
        for c in range(5):
            new = load_columns(spike_ref, 25 * i + 5 * c, 1)[0]
            out += vadd(sums[5 * c : 5 * c + 5], matvec(chain, new))
        for c in range(5):
            new = load_columns(factor_ref, 25 * i + 5 * c, 1)[0]
            store_columns(chain_ref, 25 * i + 5 * c, [matvec(chain, new)])
        return out

    sums = lax.fori_loop(1, rows, inner, flatten(load_columns(spike_ref, 0, 5)))
    cell = load_cell(cell_ref, 0)
    top = [sums[5 * c : 5 * c + 5] for c in range(5)]
    top += load_columns(chain_ref, 25 * (rows - 1), 5)
    side = [[-e for e in to_conserved(advect(col, cell[0] - eps, cell[5]), cell)] for col in top]
    emit_list(keep_ref, send_ref, place_bit(0), flatten(side))


def right_kernel(
    rows, half, state_ref, cell_ref, lu_ref, chain_ref, left_ref, right_ref,
    part_ref, keep_ref, send_ref, halo_ref,
):
    planes = state_ref.shape[1] // rows
    lanes = state_ref.shape[2]
    diag, eps, scale = DIAGONAL / half, DAMPING / half, 1.0 / half
    lane = lax.broadcasted_iota(jnp.int32, (planes, lanes), 1)
    plane = lax.broadcasted_iota(jnp.int32, (planes, lanes), 0)
    for side, ref in enumerate((right_ref, left_ref)):
        fields = [ref[c] for c in range(5)]
        for c, value in enumerate(flux_along(fields, primitives(fields), 2)):
            halo_ref[5 * side + c] = value

    def prepare(i, carry):
        fields = load_state(state_ref, i, planes, rows)
        cell = load_cell(cell_ref, i)
        own = flux_along(fields, cell, 2)
        after = lax.rem(lanes - EDGE * i, lanes)
        before = lanes - EDGE * (i + 1)
        normal = flux_along(fields, cell, 3)
        q = []
        for c in range(5):
            above = pltpu.roll(halo_ref[c], after, 1)
            below = pltpu.roll(halo_ref[5 + c], before, 1)
            plus1 = pltpu.roll(jnp.where(lane < 1, above, own[c]), lanes - 1, 1)
            plus2 = pltpu.roll(jnp.where(lane < 2, above, own[c]), lanes - 2, 1)
            less1 = pltpu.roll(jnp.where(lane >= lanes - 1, below, own[c]), 1, 1)
            less2 = pltpu.roll(jnp.where(lane >= lanes - 2, below, own[c]), 2, 1)
            span = (less2 - plus2 + 8.0 * (plus1 - less1)) / 12.0
            mirror = normal[c] if c == 3 else -normal[c]
            below = jnp.where(plane == 0, mirror, pltpu.roll(normal[c], 1, 0))
            above = jnp.where(plane == planes - 1, normal[c], pltpu.roll(normal[c], planes - 1, 0))
            q.append(-span - 0.5 * (above - below))
        right = to_primitive(q, cell)
        right[0] = right[0] + fields[0]
        right[4] = right[4] + cell[4]
        for c in range(5):
            part_ref[5 * i + c] = right[c] * scale
        return carry

    lax.fori_loop(0, rows, prepare, 0)
    part = [e * (1.0 / diag) for e in load_columns(part_ref, 0, 1)[0]]
    store_columns(part_ref, 0, [part])

    def inner(i, carry):
        part, const = carry[:5], carry[5:]
        before, here = load_cell(cell_ref, i - 1), load_cell(cell_ref, i)
        moved = shift_frame(
            advect(part, before[0] + eps, before[5]), differences(here, before)
        )
        lu = load_columns(lu_ref, 25 * i, 5)
        factors = lu, [lu[r][r] for r in range(5)]
        part = resolve(factors, vadd(load_columns(part_ref, 5 * i, 1)[0], moved))
        store_columns(part_ref, 5 * i, [part])
        const = vadd(const, matvec(load_columns(chain_ref, 25 * (i - 1), 5), part))
        return part + const

    end = rows - 1
    carry = lax.fori_loop(1, rows, inner, part + part)
    part, const = carry[:5], carry[5:]
    first_cell, last_cell = load_cell(cell_ref, 0), load_cell(cell_ref, end)
    const1 = to_conserved(advect(part, last_cell[0] + eps, last_cell[5]), last_cell)
    const0 = to_conserved(advect(const, first_cell[0] - eps, first_cell[5]), first_cell)
    values = [-e for e in const0] + const1
    values += load_state(state_ref, 0, planes, rows) + load_state(state_ref, end, planes, rows)
    emit_list(keep_ref, send_ref, place_bit(0), values)


def finish_kernel(
    rows, half, state_ref, factor_ref, spike_ref, part_ref, kept_ref, came_ref,
    next_ref, flux_ref,
):
    planes = state_ref.shape[1] // rows
    eps = DAMPING / half
    bit = place_bit(0)
    mine = [join_halves(kept_ref[e], came_ref[e], bit, planes) for e in range(20)]
    low_in, high_in, low_n, high_n = (mine[5 * g : 5 * g + 5] for g in range(4))

    load = load_columns

    def step(k, carry):
        i = rows - 1 - k
        w, flux1, flux2 = carry
        spike, factor = load(spike_ref, 25 * i, 5), load(factor_ref, 25 * i, 5)
        part = load(part_ref, 5 * i, 1)[0]
        w = vadd(vadd(part, matvec(spike, low_in)), matvec(factor, w))
        fields = [state_ref[c, pl.ds(i, planes, stride=rows), :] for c in range(5)]
        u, v, speed_w, kinetic, pressure, inverse = primitives(fields)
        cell = (u, v, speed_w, kinetic)
        value = to_conserved(w, cell)
        flux0 = to_conserved(advect(w, u, GAMMA * pressure * inverse), cell)
        for c in range(5):
            next_ref[c, pl.ds(i, planes, stride=rows), :] = value[c]

        @pl.when(k > 0)
        def _():
            for c in range(5):
                flux_ref[c, pl.ds(i + 1, planes, stride=rows), :] = 0.5 * (flux0[c] - flux2[c])

        return w, flux0, flux1

    outer = [eps * n - g for n, g in zip(high_n, high_in)]
    zero = [jnp.zeros_like(e) for e in outer]
    _, flux1, flux2 = lax.fori_loop(0, rows, step, (high_in, outer, zero))
    inner = [g - eps * n for n, g in zip(low_n, low_in)]
    for c in range(5):
        flux_ref[c, pl.ds(0, planes, stride=rows), :] = 0.5 * (inner[c] - flux2[c])


def call(kernel, out_shapes, scratch=()):
    vmem = pl.BlockSpec(memory_space=pltpu.VMEM)

    def run(*args):
        return pl.pallas_call(
            kernel,
            out_shape=[jax.ShapeDtypeStruct(s, jnp.float32) for s in out_shapes],
            in_specs=[vmem] * len(args),
            out_specs=[vmem] * len(out_shapes),
            compiler_params=pltpu.CompilerParams(vmem_limit_bytes=16 << 20),
            scratch_shapes=[pltpu.VMEM(s, jnp.float32) for s in scratch],
        )(*args)

    return run


def on_device(state):
    fields, planes, rows, lanes = state.shape
    half = 0.5 * 4.0 * rows
    eps = DAMPING / half
    size = lax.axis_size("stream")
    levels = size.bit_length() - 1
    flat = (fields, planes * rows, lanes)
    tile = (planes, lanes)
    store = (25 * rows, *tile)
    edge = (fields, *tile)
    shapes = [tile]
    for _ in range(levels - 1):
        shapes.append(half_shape(shapes[-1]))
    lines = shapes[-1]
    halves = lambda n: [(n, *shapes[1])] * 2

    def swap(array, level):
        return lax.ppermute(array, "stream", [(s, s ^ (1 << level)) for s in range(size)])

    state_rows = state.reshape(flat)
    factor, spike, lu, cells, head, tail, own1, sent1 = call(
        functools.partial(sweep_kernel, rows, half),
        [store, store, store, (CELL * rows, *tile), edge, edge] + halves(MATRIX),
    )(state_rows)
    span = lax.axis_size("span")
    up = [(i, (i + 1) % span) for i in range(span)]
    with jax.named_scope("halo_up"):
        left = lax.ppermute(tail, "span", up)
    with jax.named_scope("halo_down"):
        right = lax.ppermute(head, "span", [(j, i) for i, j in up])
    with jax.named_scope("swap_side1"):
        came1 = swap(sent1, 0)
    with jax.named_scope("chain"):
        chain, own0, sent0 = call(
            functools.partial(chain_kernel, rows, half), [store] + halves(MATRIX)
        )(factor, spike, cells)
    with jax.named_scope("swap_side0"):
        came0 = swap(sent0, 0)
    with jax.named_scope("right"):
        part, own2, sent2 = call(
            functools.partial(right_kernel, rows, half),
            [(5 * rows, *tile)] + halves(VECTOR),
            [(10, *tile)],
        )(state_rows, cells, lu, chain, left, right)
    came2 = swap(sent2, 0)
    own, came = [own0, own1, own2], [came0, came1, came2]
    sizes = [MATRIX, MATRIX, VECTOR]
    faces = []
    for level in range(levels - 2):
        kept, sent, face = call(
            functools.partial(merge_kernel, level, level == levels - 3, sizes),
            [(PORT, *shapes[level + 2])] * 2 + [(PORT, *shapes[level + 1])],
        )(*own, *came)
        faces.append(face)
        own, came, sizes = [kept], [swap(sent, level + 1)], [PORT]
    face, opened, sent = call(
        functools.partial(inner_kernel, levels - 2), [(70, *lines), (35, *lines), (35, *lines)]
    )(*own, *came)
    came = swap(sent, levels - 1)
    own, sent = call(
        functools.partial(middle_kernel, levels - 1, eps), [(20, *lines)] * 2
    )(opened, came, face)
    for level in reversed(range(levels - 2)):
        came = swap(sent, level + 1)
        own, sent = call(
            functools.partial(down_kernel, level, eps, shapes[level + 1][0]),
            [(20, *shapes[level + 1])] * 2,
        )(own, came, faces[level])
    came = swap(sent, 0)
    state_next, flux_difference = call(
        functools.partial(finish_kernel, rows, half), [flat, flat]
    )(state_rows, factor, spike, part, own, came)
    return state_next.reshape(state.shape), flux_difference.reshape(state.shape)


def solution(mesh):
    spec = P(None, None, "stream", "span")
    return jax.shard_map(
        on_device, mesh=mesh, in_specs=(spec,), out_specs=(spec, spec), check_vma=False
    )
```
